32 devices in a mesh: sec: 8 (over y, x, core), col: 4 (over z).
Axes of the slice: x: 2, y: 2, z: 4, core: 2. Of those that a mesh axis runs over, the one named last changes fastest.
Arguments:
- air_state: float32 [4, 64, 32768], P(None, None, ('sec', 'col')), may hold values from -6 to 6
- air_mix: float32 [64, 32768], P(None, ('sec', 'col')), may hold values from 0.1 to 4
- surface_forcing: float32 [4, 32768], P(None, ('sec', 'col')), may hold values from 0 to 2
- air_mask: int32 [32768], P(('sec', 'col')), may hold values 0 or 1
- ocean_sources: int32 [4, 32768], P(None, ('sec', 'col')), may hold values from 0 to 6143, as said below
- ocean_weights: float32 [4, 32768], P(None, ('sec', 'col')), may hold values from 0.1 to 0.5
- sea_state: float32 [2, 80, 16384], P(None, None, ('sec', 'col')), may hold values from -6 to 6
- sea_mix: float32 [80, 16384], P(None, ('sec', 'col')), may hold values from 0.1 to 4
- ice_cover: float32 [16384], P(('sec', 'col')), may hold values from 0.05 to 0.95
- sea_mask: int32 [16384], P(('sec', 'col')), may hold values 0 or 1
- air_sources: int32 [4, 16384], P(None, ('sec', 'col')), may hold values from 0 to 12287, as said below
- air_weights: float32 [4, 16384], P(None, ('sec', 'col')), may hold values from 0.1 to 0.5
Outputs:
- air_out: float32 [4, 64, 32768], P(None, None, ('sec', 'col'))
- sea_out: float32 [2, 80, 16384], P(None, None, ('sec', 'col'))
- ice_out: float32 [16384], P(('sec', 'col'))
The draws below stay inside these ranges and needn't reach their ends.
Inputs may be any that keep to these rules, and one draw needn't show every extreme that they name: Section t holds ocean cells t * 2048 to (t + 1) * 2048 - 1 and atmosphere columns t * 4096 to (t + 1) * 4096 - 1. An entry s of ocean_sources names cell s mod 2048 of the section s // 2048 - 1 places after the column's own. An entry s of air_sources names column s mod 4096 of the section s // 4096 - 1 places after the cell's own.
All inputs are finite; a program needn't handle non-finite values. No bound on the sum of `air_mask` or of `sea_mask` on one device may be relied on, other than what follows from the above.
Results may differ from the reference program's by a relative error of at most 0.0001.
Values sent between devices are 32-bit elements; how exact they have to be, the bound alone decides.
No kernel may reach another device: no remote copies, remote signals or barrier semaphores. Data moves between devices by JAX's collectives and lax.ppermute only.
A program may use at most 64 MiB of HBM per device.

```python
import math
import jax
import jax.numpy as jnp
from jax import lax

LEV = 64
OLEV = 80
KA = 4
KO = 4
STEPS = 2
SECA = 4096
SECO = 2048
ACOLS = 32768
OCELLS = 16384


def draw_ocean_sources(key, part):
    key_band, key_cell = jax.random.split(jax.random.fold_in(key, 17))
    offset = jax.random.randint(key_band, (KO, ACOLS), 0, 3)
    within = jax.random.randint(key_cell, (KO, ACOLS), 0, SECO)
    return (offset * SECO + within).astype(jnp.int32)


def draw_air_sources(key, part):
    key_band, key_cell = jax.random.split(jax.random.fold_in(key, 29))
    offset = jax.random.randint(key_band, (KA, OCELLS), 0, 3)
    within = jax.random.randint(key_cell, (KA, OCELLS), 0, SECA)
    return (offset * SECA + within).astype(jnp.int32)


def set_ends(drawn, key, smallest, top_value):
    longest = drawn.shape.index(max(drawn.shape))
    spots = []
    for shift in (0, 1):
        where = [jax.random.randint(jax.random.fold_in(key, axis), (), 0, length) for axis, length in enumerate(drawn.shape)]
        where[longest] = (where[longest] + shift) % drawn.shape[longest]
        spots.append(tuple(where))
    return drawn.at[spots[0]].set(smallest).at[spots[1]].set(top_value)


def block_scale(key, shape, shards, least, largest):
    gain, own = 1.0, jax.random.fold_in(key, 6)
    for dim, shards_of in shards:
        draws = jnp.exp(jax.random.uniform(jax.random.fold_in(own, dim), (shards_of,), jnp.float32, least / len(shards), largest / len(shards)))
        gain = gain * jnp.repeat(draws, shape[dim] // shards_of).reshape([-1 if axis == dim else 1 for axis in range(len(shape))])
    return gain


def bell_draw(stream_key, extent, deviation, reach, cuts=(), kind=jnp.bfloat16):
    drawn = deviation * jax.random.normal(stream_key, extent, jnp.float32)
    if cuts:
        drawn = drawn * block_scale(stream_key, extent, cuts, -0.22, 0.18)
    return jnp.clip(drawn, -reach, reach).astype(kind)


def setup_inputs(seed: int = 0) -> dict:
    keys = jax.random.split(jax.random.key(seed), 13)
    air_state = bell_draw(keys[0], (4, LEV, ACOLS), 1.0, 6.0, ((2, 32),), jnp.float32)
    air_mix = jnp.clip(jnp.exp(math.log(4.0) - 3.6888794 * jax.random.uniform(keys[1], (LEV, ACOLS), jnp.float32) ** block_scale(keys[1], (LEV, ACOLS), ((1, 32),), -0.2, 0.2)), 0.1, 4.0)
    surface_forcing = jnp.clip(2.0 * jax.random.uniform(keys[2], (4, ACOLS), jnp.float32) ** block_scale(keys[2], (4, ACOLS), ((1, 32),), -0.2, 0.2), 0.0, 2.0)
    air_mask = set_ends((jax.random.randint(keys[3], (ACOLS,), 0, 3) < 2).astype(jnp.int32), jax.random.fold_in(keys[3], 1), 0, 1)
    ocean_sources = draw_ocean_sources(jax.random.fold_in(keys[12], 71), 0)
    ocean_weights = jnp.clip(0.1 + 0.4 * jax.random.uniform(keys[5], (KO, ACOLS), jnp.float32) ** block_scale(keys[5], (KO, ACOLS), ((1, 32),), -0.2, 0.2), 0.1, 0.5)
    sea_state = bell_draw(keys[6], (2, OLEV, OCELLS), 1.0, 6.0, ((2, 32),), jnp.float32)
    sea_mix = jnp.clip(jnp.exp(math.log(4.0) - 3.6888794 * jax.random.uniform(keys[7], (OLEV, OCELLS), jnp.float32) ** block_scale(keys[7], (OLEV, OCELLS), ((1, 32),), -0.2, 0.2)), 0.1, 4.0)
    ice_cover = jnp.clip(0.05 + 0.9 * jax.random.uniform(keys[8], (OCELLS,), jnp.float32) ** block_scale(keys[8], (OCELLS,), ((0, 32),), -0.2, 0.2), 0.05, 0.95)
    sea_mask = set_ends((jax.random.randint(keys[9], (OCELLS,), 0, 4) < 3).astype(jnp.int32), jax.random.fold_in(keys[9], 1), 0, 1)
    air_sources = draw_air_sources(jax.random.fold_in(keys[12], 71), 0)
    air_weights = jnp.clip(0.1 + 0.4 * jax.random.uniform(keys[11], (KA, OCELLS), jnp.float32) ** block_scale(keys[11], (KA, OCELLS), ((1, 32),), -0.2, 0.2), 0.1, 0.5)
    return dict(air_state=air_state, air_mix=air_mix, surface_forcing=surface_forcing, air_mask=air_mask, ocean_sources=ocean_sources, ocean_weights=ocean_weights, sea_state=sea_state, sea_mix=sea_mix, ice_cover=ice_cover, sea_mask=sea_mask, air_sources=air_sources, air_weights=air_weights)


def solve_columns(mixing, right_side):
    column_depth = mixing.shape[0]
    zeros_row = jnp.zeros_like(mixing[0])
    carry_c = zeros_row
    carry_d = jnp.zeros_like(right_side[:, 0])
    ratios = []
    reduced = []
    for depth_index in range(column_depth):
        lower_k = mixing[depth_index - 1] if depth_index > 0 else zeros_row
        upper_k = mixing[depth_index]
        pivot_value = 1.0 + lower_k + upper_k + lower_k * carry_c
        carry_c = -upper_k / pivot_value
        carry_d = (right_side[:, depth_index] + lower_k * carry_d) / pivot_value
        ratios.append(carry_c)
        reduced.append(carry_d)
    current = reduced[-1]
    solved = [current]
    for depth_index in range(column_depth - 2, -1, -1):
        current = reduced[depth_index] - ratios[depth_index] * current
        solved.append(current)
    return jnp.stack(solved[::-1], axis=1)

def global_places(sources, home_span, source_span, section_count):
    owners = jnp.arange(sources.shape[1], dtype=jnp.int32) // home_span
    band = jnp.mod(owners[None, :] - 1 + sources // source_span, section_count)
    return (band * source_span + sources % source_span).astype(jnp.int32)

def remap(values, sources, weights):
    return lax.optimization_barrier(jnp.sum(weights[None] * values[:, sources], axis=1))

def surface_fluxes(air_state, air_sea, surface_forcing, air_mask):
    bottom = air_state[:, 0]
    over_sea = air_mask == 1
    skin = jnp.where(over_sea, air_sea[0], surface_forcing[3])
    frozen = jnp.where(over_sea, air_sea[1], 0.0)
    speed = jnp.sqrt(bottom[2] * bottom[2] + bottom[3] * bottom[3] + 1.0)
    coefficient = 0.3 * speed / (1.0 + frozen)
    snow_part = 1.0 / (1.0 + jnp.exp(2.0 * skin))
    return jnp.stack([coefficient * (skin - bottom[0]), coefficient * (0.5 * jnp.exp(0.3 * skin) - bottom[1]), coefficient * bottom[2], coefficient * bottom[3], surface_forcing[0] / (1.0 + frozen), surface_forcing[1] - 0.2 * skin, surface_forcing[2] * (1.0 - snow_part), surface_forcing[2] * snow_part])

def air_step(air_state, air_mix, fluxes):
    bottom_add = jnp.stack([fluxes[0], fluxes[1], -fluxes[2], -fluxes[3]])
    return solve_columns(air_mix, air_state.at[:, 0].add(bottom_add))

def sea_step(sea_state, sea_mix, ice_cover, sea_mask, sea_flux):
    stress = jnp.sqrt(sea_flux[2] * sea_flux[2] + sea_flux[3] * sea_flux[3] + 0.01)
    heat = sea_flux[4] + sea_flux[5] - sea_flux[0] - sea_flux[1]
    open_water = 1.0 - ice_cover
    depth_decay = jnp.exp(-jnp.arange(sea_mix.shape[0], dtype=jnp.float32) / 8.0)
    mixing = sea_mix * (1.0 + 2.0 * stress[None, :] * depth_decay[:, None])
    top_add = jnp.stack([0.5 * open_water * heat, 0.3 * open_water * (0.4 * sea_flux[1] - sea_flux[6])])
    solved = solve_columns(mixing, sea_state.at[:, 0].add(top_add))
    wet_cells = sea_mask == 1
    new_state = jnp.where(wet_cells[None, None], solved, sea_state)
    grown = ice_cover / (ice_cover + open_water * jnp.exp(0.5 * heat - 0.8 * sea_flux[7]))
    return (new_state, jnp.where(wet_cells, grown, ice_cover))

def reference(air_state, air_mix, surface_forcing, air_mask, ocean_sources, ocean_weights, sea_state, sea_mix, ice_cover, sea_mask, air_sources, air_weights):
    section_count = ACOLS // SECA
    ocean_cell = global_places(ocean_sources, SECA, SECO, section_count)
    air_column = global_places(air_sources, SECO, SECA, section_count)
    for step_index in range(STEPS):
        sea_top = jnp.stack([sea_state[0, 0], ice_cover])
        air_sea = remap(sea_top, ocean_cell, ocean_weights)
        fluxes = surface_fluxes(air_state, air_sea, surface_forcing, air_mask)
        air_state = air_step(air_state, air_mix, fluxes)
        sea_flux = remap(fluxes, air_column, air_weights)
        sea_state, ice_cover = sea_step(sea_state, sea_mix, ice_cover, sea_mask, sea_flux)
    return (air_state, sea_state, ice_cover)
```

```python
import math

import jax
import jax.numpy as jnp
from jax import lax
from jax.experimental import pallas as pl
from jax.experimental.pallas import tpu as pltpu
from jax.sharding import PartitionSpec as P

STEPS = 2
LANES = 128
SUBS = 8
FLUXES = 5


def tile_rows(x):
    *lead, r, n = x.shape
    t = min(r, SUBS)
    y = x.reshape(*lead, r // t, t, n // LANES, LANES)
    return jnp.swapaxes(y, -3, -2).reshape(*lead, r * n // LANES, LANES)


def untile_rows(x, r, n):
    lead = x.shape[:-2]
    t = min(r, SUBS)
    y = x.reshape(*lead, r // t, n // LANES, t, LANES)
    return jnp.swapaxes(y, -3, -2).reshape(*lead, r, n)


def level_rows(level, tiles, height=SUBS):
    return pl.ds((level // height) * height * tiles + level % height, tiles, stride=height)


def split(x, size):
    if size & (size - 1) == 0:
        return x >> (size.bit_length() - 1), x & (size - 1)
    return x // size, x % size


def sec_partners():
    n = lax.axis_size("sec")
    if n % 2 == 0:
        return (
            [(i, i ^ 1) for i in range(n)],
            [(i, (i + 1) % n if i % 2 else (i - 1) % n) for i in range(n)],
        )
    return ([(i, (i + 1) % n) for i in range(n)], [(i, (i - 1) % n) for i in range(n)])


def section_slot(band, sec, n):
    odd = sec & 1 if n % 2 == 0 else 1
    return jnp.where(band == 1, 0, jnp.where((band == 0) == (odd == 1), 1, 2))


def col_pairs(j):
    n = lax.axis_size("col")
    if n & (n - 1) == 0:
        return [(i, i ^ j) for i in range(n)]
    return [(i, (i + j) % n) for i in range(n)]


def row_slot(owner, col, n):
    if n & (n - 1) == 0:
        return owner ^ col
    rest = col - owner
    return jnp.where(rest < 0, rest + n, rest)


def sec_exchange(x):
    return [lax.ppermute(x, "sec", pairs) for pairs in sec_partners()]


def factor(mix, depth, put):
    half = depth // 2
    one = jnp.ones_like(mix(0))
    sides = []
    for side in (0, 1):
        if side == 0:
            sides.append([one, one, None])
        else:
            sides.append([one + mix(depth - 1), one, None])
    scale = [None, None]
    last = [None, None]
    for step in range(half):
        for side in (0, 1):
            n, d, _ = sides[side]
            i = step if side == 0 else depth - 1 - step
            ahead = mix(i) if side == 0 else mix(i - 1)
            behind = None
            if step:
                behind = mix(i - 1) if side == 0 else mix(i)
            d1 = n + ahead * d
            r1 = 1.0 / d1
            inv = d * r1
            n1 = d1 + ahead * n
            if step % 4 == 3:
                d1, n1 = d1 * scale[side], n1 * scale[side]
            if step % 4 == 0:
                scale[side] = r1
            out = ahead * inv
            put(i, inv, out, None if behind is None else behind * inv)
            sides[side] = [n1, d1, None]
            last[side] = out
    return 1.0 / (1.0 - last[0] * last[1])


def apply_factor(rhs, depth, get, middle, keep, kept, store):
    half = depth // 2
    carry = [None, None]
    for step in range(half):
        for side in (0, 1):
            i = step if side == 0 else depth - 1 - step
            inv, _, back = get(i)
            r = rhs(i)
            value = None if r is None else r * inv
            if step and carry[side] is not None:
                moved = back * carry[side]
                value = moved if value is None else value + moved
            carry[side] = value
            if value is not None:
                keep(i, value)
    top, bottom = carry
    up, down = get(half - 1)[1], get(half)[1]
    x_top = (top if bottom is None else top + up * bottom) * middle
    x_bottom = down * x_top if bottom is None else bottom + down * x_top
    store(half - 1, x_top)
    store(half, x_bottom)
    xs = [x_top, x_bottom]
    for step in range(half - 2, -1, -1):
        for side in (0, 1):
            i = step if side == 0 else depth - 1 - step
            x = get(i)[1] * xs[side]
            if side == 0 or bottom is not None:
                x = x + kept(i)
            xs[side] = x
            store(i, x)


def air_prepare(cols, secs, cells_here, air_ref, mix_ref, src_ref, w_ref, forcing_ref, mask_ref,
                y2_ref, hg_ref, top_ref, code_ref, fixed_ref, fac, work, x1):
    depth = fac.shape[1]
    tiles = mix_ref.shape[0] // depth
    fields = air_ref.shape[0]
    sec, col = lax.axis_index("sec"), lax.axis_index("col")

    mask = mask_ref[...] == 1
    ks = src_ref.shape[0] // tiles
    for k in range(ks):
        s = src_ref[pl.ds(k, tiles, stride=ks), :]
        band, within = split(s, cells_here * cols)
        owner, place = split(within, cells_here)
        slot = section_slot(band, sec, secs) * cols + row_slot(owner, col, cols)
        code_ref[k] = slot * cells_here + place
        fixed_ref[k] = jnp.where(mask, w_ref[pl.ds(k, tiles, stride=ks), :], 0.0)
    nf = forcing_ref.shape[0] // tiles
    for k in range(nf):
        f = forcing_ref[pl.ds(k, tiles, stride=nf), :]
        fixed_ref[ks + k] = f if k < nf - 1 else jnp.where(mask, 0.0, f)
    for f in range(fields):
        fixed_ref[ks + nf + f] = air_ref[f, level_rows(0, tiles), :]

    def put(i, inv, out, back):
        fac[0, i] = inv
        fac[1, i] = out
        if back is not None:
            fac[2, i] = back

    middle = factor(lambda i: mix_ref[level_rows(i, tiles), :], depth, put)

    class Get:
        def __call__(self, i):
            return (fac[0, i], fac[1, i], fac[2, i])

    get = Get()
    for f in range(fields + 1):
        def rhs(i, f=f):
            if f < fields:
                return air_ref[f, level_rows(i, tiles), :]
            return jnp.ones_like(middle) if i == 0 else None

        def keep(i, v, f=f):
            work[f, i] = v

        def kept(i, f=f):
            return work[f, i]

        def store(i, v, f=f):
            x1[f, i] = v
            if f == fields:
                hg_ref[1, level_rows(i, tiles), :] = v

        apply_factor(rhs, depth, get, middle, keep, kept, store)
        top_ref[f] = x1[f, 0]
    for f in range(fields + 1):
        def rhs(i, f=f):
            return x1[f, i]

        def keep(i, v, f=f):
            work[f, i] = v

        def kept(i, f=f):
            return work[f, i]

        def store(i, v, f=f):
            if f < fields:
                y2_ref[f, level_rows(i, tiles), :] = v
            else:
                hg_ref[0, level_rows(i, tiles), :] = v

        apply_factor(rhs, depth, get, middle, keep, kept, store)


def first_bundle(cols, secs, cols_here, own_ref, m1_ref, m2_ref, src_ref, w_ref, out_ref):
    sec = lax.axis_index("sec")
    n = own_ref.shape[0]
    out_ref[0:n] = own_ref[...]
    out_ref[n : 2 * n] = m1_ref[...]
    out_ref[2 * n : 3 * n] = m2_ref[...]
    s = src_ref[...]
    band, within = split(s, cols_here * cols)
    owner, place = split(within, cols_here)
    code = (owner * 3 + section_slot(band, sec, secs)) * cols_here + place
    m = s.shape[0]
    out_ref[3 * n : 3 * n + m] = code.astype(jnp.float32)
    out_ref[3 * n + m : 3 * n + 2 * m] = w_ref[...]


def later_bundle(own_ref, m1_ref, m2_ref, out_ref):
    n = own_ref.shape[0]
    out_ref[0:n] = own_ref[...]
    out_ref[n : 2 * n] = m1_ref[...]
    out_ref[2 * n : 3 * n] = m2_ref[...]


def lane_gather(row, lane):
    return jnp.take_along_axis(jnp.broadcast_to(row, lane.shape), lane, axis=1)


def flux_kernel(later, pieces, cell_rows, *refs):
    tables, refs = refs[:pieces], refs[pieces:]
    code_ref, fixed_ref, refs = refs[0], refs[1], refs[2:]
    if later:
        top_ref, before_ref, refs = refs[0], refs[1], refs[2:]
    flux_ref, add_ref = refs
    ks = code_ref.shape[0]
    his, lanes, vals = [], [], []
    for k in range(ks):
        hi, lane = split(code_ref[k], LANES)
        his.append(hi)
        lanes.append(lane)
        vals.append([jnp.zeros(lane.shape, jnp.float32) for _ in range(2)])
    for slot in range(3):
        for j in range(pieces):
            for r in range(cell_rows):
                number = (slot * pieces + j) * cell_rows + r
                base = slot * 2 * cell_rows + r
                row0 = tables[j][base : base + 1, :]
                row1 = tables[j][base + cell_rows : base + cell_rows + 1, :]
                for k in range(ks):
                    hit = his[k] == number
                    vals[k][0] = jnp.where(hit, lane_gather(row0, lanes[k]), vals[k][0])
                    vals[k][1] = jnp.where(hit, lane_gather(row1, lanes[k]), vals[k][1])
    skin = fixed_ref[ks + 3]
    frozen = jnp.zeros_like(skin)
    for k in range(ks):
        skin = skin + fixed_ref[k] * vals[k][0]
        frozen = frozen + fixed_ref[k] * vals[k][1]
    bottom = [fixed_ref[ks + 4 + f] for f in range(4)]
    if later:
        g = top_ref[4]
        bottom = [top_ref[f] + g * before_ref[f] for f in range(4)]
    short, long_, rain = fixed_ref[ks], fixed_ref[ks + 1], fixed_ref[ks + 2]
    cover = 1.0 / (1.0 + frozen)
    speed = jnp.sqrt(bottom[2] * bottom[2] + bottom[3] * bottom[3] + 1.0)
    coefficient = 0.3 * speed * cover
    snow = 1.0 / (1.0 + jnp.exp(2.0 * skin))
    f0 = coefficient * (skin - bottom[0])
    f1 = coefficient * (0.5 * jnp.exp(0.3 * skin) - bottom[1])
    f2 = coefficient * bottom[2]
    f3 = coefficient * bottom[3]
    f4 = short * cover
    f5 = long_ - 0.2 * skin
    f6 = rain * (1.0 - snow)
    f7 = rain * snow
    n = skin.shape[0]
    for v, value in enumerate((f2, f3, f4 + f5 - f0 - f1, 0.4 * f1 - f6, f7)):
        flux_ref[v * n : (v + 1) * n] = value
    for v, value in enumerate((f0, f1, -f2, -f3)):
        add_ref[v] = value


def partial_kernel(pieces, cell_rows, offset, *refs):
    flux, refs = refs[:3], refs[3:]
    bundles, outs = refs[:pieces], refs[pieces:]
    col_rows = flux[0].shape[0] // FLUXES
    base = lax.axis_index("col") * (3 * col_rows)
    m = outs[0].shape[0] // FLUXES
    ks = (bundles[0].shape[0] - offset) // 2 // m
    per = SUBS // m
    for j in range(pieces):
        total = [None] * FLUXES
        for q in range(ks // per):
            code, w = [], []
            for k in range(q * per, (q + 1) * per):
                code.append(bundles[j][pl.ds(offset + k, m, stride=ks), :])
                w.append(bundles[j][pl.ds(offset + ks * m + k, m, stride=ks), :])
            code = jnp.concatenate(code, axis=0).astype(jnp.int32)
            w = jnp.concatenate(w, axis=0)
            hi, lane = split(code, LANES)
            hi = hi - base
            vals = [jnp.zeros(lane.shape, jnp.float32) for _ in range(FLUXES)]
            for slot in range(3):
                for r in range(col_rows):
                    hit = hi == slot * col_rows + r
                    for v in range(FLUXES):
                        row = flux[slot][v * col_rows + r : v * col_rows + r + 1, :]
                        vals[v] = jnp.where(hit, lane_gather(row, lane), vals[v])
            for v in range(FLUXES):
                part = w * vals[v]
                total[v] = part if total[v] is None else total[v] + part
        for v in range(FLUXES):
            whole = total[v][0:m]
            for p in range(1, per):
                whole = whole + total[v][p * m : (p + 1) * m]
            outs[j][v * m : (v + 1) * m] = whole


def sea_kernel(pieces, depth, last, *refs):
    parts, refs = refs[:pieces], refs[pieces:]
    state_ref, mix_ref, ice_ref, mask_ref, refs = refs[0], refs[1], refs[2], refs[3], refs[4:]
    out_ref, top_ref, fac, work = refs
    tiles = mix_ref.shape[0] // depth
    flux = []
    for v in range(FLUXES):
        total = parts[0][v * tiles : (v + 1) * tiles]
        for p in parts[1:]:
            total = total + p[v * tiles : (v + 1) * tiles]
        flux.append(total)
    ice = ice_ref[...]
    wet = mask_ref[...] == 1
    stress2 = 2.0 * jnp.sqrt(flux[0] * flux[0] + flux[1] * flux[1] + 0.01)
    heat, salt, snow = flux[2], flux[3], flux[4]
    open_water = 1.0 - ice
    adds = (0.5 * open_water * heat, 0.3 * open_water * salt)
    grown = ice / (ice + open_water * jnp.exp(0.5 * heat - 0.8 * snow))
    new_ice = jnp.where(wet, grown, ice)

    known = {}

    def mix(i):
        if i not in known:
            k = mix_ref[level_rows(i, tiles), :]
            known[i] = k * (1.0 + stress2 * math.exp(-i / 8.0))
        return known[i]

    def put(i, inv, out, back):
        fac[0, i] = inv
        fac[1, i] = out
        if back is not None:
            fac[2, i] = back

    middle = factor(mix, depth, put)
    for f in range(2):
        def rhs(i, f=f):
            r = state_ref[f, level_rows(i, tiles), :]
            return r + adds[f] if i == 0 else r

        def keep(i, v, f=f):
            work[f, i] = v

        def kept(i, f=f):
            return work[f, i]

        def store(i, v, f=f):
            new = jnp.where(wet, v, state_ref[f, level_rows(i, tiles), :])
            out_ref[f, level_rows(i, tiles), :] = new
            if f == 0 and i == 0 and not last:
                top_ref[0:tiles] = new

        apply_factor(rhs, depth, lambda i: (fac[0, i], fac[1, i], fac[2, i]), middle, keep, kept, store)
    if last:
        top_ref[...] = new_ice
    else:
        top_ref[tiles : 2 * tiles] = new_ice


def air_finish(y2_ref, hg_ref, first_ref, second_ref, out_ref):
    fields, tiles = first_ref.shape[0], first_ref.shape[1]
    rows = y2_ref.shape[1]
    for f in range(fields):
        for j in range(tiles):
            b1 = jnp.broadcast_to(first_ref[f, j : j + 1, :], (SUBS, LANES))
            b2 = jnp.broadcast_to(second_ref[f, j : j + 1, :], (SUBS, LANES))
            for t in range(rows // (SUBS * tiles)):
                at = slice((t * tiles + j) * SUBS, (t * tiles + j + 1) * SUBS)
                out_ref[f, at] = y2_ref[f, at] + hg_ref[0, at] * b1 + hg_ref[1, at] * b2


def call(kernel, name, out, *args, scratch=()):
    many = isinstance(out, list)
    return pl.pallas_call(
        kernel,
        name=name,
        out_shape=[jax.ShapeDtypeStruct(*o) for o in out] if many else jax.ShapeDtypeStruct(*out),
        in_specs=[pl.BlockSpec(memory_space=pltpu.VMEM)] * len(args),
        out_specs=[pl.BlockSpec(memory_space=pltpu.VMEM)] * len(out) if many else pl.BlockSpec(memory_space=pltpu.VMEM),
        scratch_shapes=list(scratch),
    )(*args)


def per_device(air_state, air_mix, surface_forcing, air_mask, ocean_sources, ocean_weights,
               sea_state, sea_mix, ice_cover, sea_mask, air_sources, air_weights):
    cols, secs = lax.axis_size("col"), lax.axis_size("sec")
    fields, levels, here = air_state.shape
    depth, cells = sea_mix.shape
    tiles, sea_tiles = here // LANES, cells // LANES
    f32, i32 = jnp.float32, jnp.int32
    ko = ocean_sources.shape[0]

    air = tile_rows(air_state)
    mixing = tile_rows(air_mix)
    sea = tile_rows(sea_state)
    sea_k = tile_rows(sea_mix)
    ice = ice_cover.reshape(sea_tiles, LANES)
    wet = sea_mask.reshape(sea_tiles, LANES)

    top = jnp.concatenate([sea_state[0, 0].reshape(sea_tiles, LANES), ice], axis=0)
    near = sec_exchange(top)
    y2, hg, tops, code, fixed = call(
        lambda *r: air_prepare(cols, secs, cells, *r), "air_prepare",
        [(air.shape, f32), ((2,) + mixing.shape, f32), ((fields + 1, tiles, LANES), f32),
         ((ko, tiles, LANES), i32), ((ko + 8, tiles, LANES), f32)],
        air, mixing, tile_rows(ocean_sources), tile_rows(ocean_weights), tile_rows(surface_forcing),
        air_mask.reshape(tiles, LANES),
        scratch=[pltpu.VMEM((3, levels, tiles, LANES), f32), pltpu.VMEM((fields + 1, levels, tiles, LANES), f32),
                 pltpu.VMEM((fields + 1, levels, tiles, LANES), f32)],
    )
    src, w = tile_rows(air_sources), tile_rows(air_weights)
    offset = 6 * sea_tiles
    bundle = call(
        lambda *r: first_bundle(cols, secs, here, *r), "first_bundle",
        ((offset + 2 * src.shape[0], LANES), f32), top, *near, src, w,
    )
    bundles = [bundle] + [lax.ppermute(bundle, "col", col_pairs(j)) for j in range(cols - 1, 0, -1)][::-1]
    adds, tables = [], bundles
    for step in range(STEPS):
        extra = (tops, adds[0]) if step else ()
        flux, add = call(
            lambda *r: flux_kernel(bool(step), cols, sea_tiles, *r), "fluxes",
            [((FLUXES * tiles, LANES), f32), ((fields, tiles, LANES), f32)],
            *tables, code, fixed, *extra,
        )
        adds.append(add)
        parts = call(
            lambda *r: partial_kernel(cols, sea_tiles, offset, *r), "partial_sums",
            [((FLUXES * sea_tiles, LANES), f32)] * cols,
            flux, *sec_exchange(flux), *bundles,
        )
        moved = [parts[0]] + [lax.ppermute(parts[j], "col", col_pairs(j)) for j in range(cols - 1, 0, -1)][::-1]
        last = step == STEPS - 1
        if last:
            air_out = call(air_finish, "air_finish", (air.shape, f32), y2, hg, *adds)
        sea, top = call(
            lambda *r: sea_kernel(cols, depth, last, *r), "sea_step",
            [(sea.shape, f32), ((sea_tiles if last else 2 * sea_tiles, LANES), f32)],
            *moved, sea, sea_k, ice, wet,
            scratch=[pltpu.VMEM((3, depth, sea_tiles, LANES), f32), pltpu.VMEM((2, depth, sea_tiles, LANES), f32)],
        )
        if not last:
            ice = top[sea_tiles:]
            bundle = call(later_bundle, "later_bundle", ((offset, LANES), f32), top, *sec_exchange(top))
            tables = [bundle] + [lax.ppermute(bundle, "col", col_pairs(j)) for j in range(cols - 1, 0, -1)][::-1]
    return (untile_rows(air_out, levels, here), untile_rows(sea, depth, cells), top.reshape(cells))


def solution(mesh):
    both = ("sec", "col")
    placed = (
        P(None, None, both), P(None, both), P(None, both), P(both), P(None, both), P(None, both),
        P(None, None, both), P(None, both), P(both), P(both), P(None, both), P(None, both),
    )
    return jax.shard_map(
        per_device,
        mesh=mesh,
        in_specs=placed,
        out_specs=(P(None, None, both), P(None, None, both), P(both)),
        check_vma=False,
    )
```

```python
import math

import jax
import jax.numpy as jnp
from jax import lax
from jax.experimental import pallas as pl
from jax.experimental.pallas import tpu as pltpu
from jax.sharding import PartitionSpec as P

STEPS = 2
LANES = 128
SUBS = 8
FLUXES = 5


def tile_rows(x):
    *lead, r, n = x.shape
    t = min(r, SUBS)
    y = x.reshape(*lead, r // t, t, n // LANES, LANES)
    return jnp.swapaxes(y, -3, -2).reshape(*lead, r * n // LANES, LANES)


def untile_rows(x, r, n):
    lead = x.shape[:-2]
    t = min(r, SUBS)
    y = x.reshape(*lead, r // t, n // LANES, t, LANES)
    return jnp.swapaxes(y, -3, -2).reshape(*lead, r, n)


def level_rows(level, tiles, height=SUBS):
    return pl.ds((level // height) * height * tiles + level % height, tiles, stride=height)


def split(x, size):
    if size & (size - 1) == 0:
        return x >> (size.bit_length() - 1), x & (size - 1)
    return x // size, x % size


def sec_partners():
    n = lax.axis_size("sec")
    if n % 2 == 0:
        return (
            [(i, i ^ 1) for i in range(n)],
            [(i, (i + 1) % n if i % 2 else (i - 1) % n) for i in range(n)],
        )
    return ([(i, (i + 1) % n) for i in range(n)], [(i, (i - 1) % n) for i in range(n)])


def section_slot(band, sec, n):
    odd = sec & 1 if n % 2 == 0 else 1
    return jnp.where(band == 1, 0, jnp.where((band == 0) == (odd == 1), 1, 2))


def col_pairs(j):
    n = lax.axis_size("col")
    if n & (n - 1) == 0:
        return [(i, i ^ j) for i in range(n)]
    return [(i, (i + j) % n) for i in range(n)]


def row_slot(owner, col, n):
    if n & (n - 1) == 0:
        return owner ^ col
    rest = col - owner
    return jnp.where(rest < 0, rest + n, rest)


def sec_exchange(x):
    return [lax.ppermute(x, "sec", pairs) for pairs in sec_partners()]


def factor(mix, depth, put):
    half = depth // 2
    one = jnp.ones_like(mix(0))
    sides = []
    for side in (0, 1):
        if side == 0:
            sides.append([one, one, None])
        else:
            sides.append([one + mix(depth - 1), one, None])
    scale = [None, None]
    last = [None, None]
    for step in range(half):
        for side in (0, 1):
            n, d, _ = sides[side]
            i = step if side == 0 else depth - 1 - step
            ahead = mix(i) if side == 0 else mix(i - 1)
            behind = None
            if step:
                behind = mix(i - 1) if side == 0 else mix(i)
            d1 = n + ahead * d
            r1 = 1.0 / d1
            inv = d * r1
            n1 = d1 + ahead * n
            if step % 4 == 3:
                d1, n1 = d1 * scale[side], n1 * scale[side]
            if step % 4 == 0:
                scale[side] = r1
            out = ahead * inv
            put(i, inv, out, None if behind is None else behind * inv)
            sides[side] = [n1, d1, None]
            last[side] = out
    return 1.0 / (1.0 - last[0] * last[1])


def apply_factor(rhs, depth, get, middle, keep, kept, store):
    half = depth // 2
    carry = [None, None]
    for step in range(half):
        for side in (0, 1):
            i = step if side == 0 else depth - 1 - step
            inv, _, back = get(i)
            r = rhs(i)
            value = None if r is None else r * inv
            if step and carry[side] is not None:
                moved = back * carry[side]
                value = moved if value is None else value + moved
            carry[side] = value
            if value is not None:
                keep(i, value)
    top, bottom = carry
    up, down = get(half - 1)[1], get(half)[1]
    x_top = (top if bottom is None else top + up * bottom) * middle
    x_bottom = down * x_top if bottom is None else bottom + down * x_top
    store(half - 1, x_top)
    store(half, x_bottom)
    xs = [x_top, x_bottom]
    for step in range(half - 2, -1, -1):
        for side in (0, 1):
            i = step if side == 0 else depth - 1 - step
            x = get(i)[1] * xs[side]
            if side == 0 or bottom is not None:
                x = x + kept(i)
            xs[side] = x
            store(i, x)


def air_prepare(cols, secs, cells_here, air_ref, mix_ref, src_ref, w_ref, forcing_ref, mask_ref,
                y2_ref, hg_ref, top_ref, code_ref, fixed_ref, fac, work, x1):
    depth = fac.shape[1]
    tiles = mix_ref.shape[0] // depth
    fields = air_ref.shape[0]
    sec, col = lax.axis_index("sec"), lax.axis_index("col")

    mask = mask_ref[...] == 1
    ks = src_ref.shape[0] // tiles
    for k in range(ks):
        s = src_ref[pl.ds(k, tiles, stride=ks), :]
        band, within = split(s, cells_here * cols)
        owner, place = split(within, cells_here)
        slot = section_slot(band, sec, secs) * cols + row_slot(owner, col, cols)
        code_ref[k] = slot * cells_here + place
        fixed_ref[k] = jnp.where(mask, w_ref[pl.ds(k, tiles, stride=ks), :], 0.0)
    nf = forcing_ref.shape[0] // tiles
    for k in range(nf):
        f = forcing_ref[pl.ds(k, tiles, stride=nf), :]
        fixed_ref[ks + k] = f if k < nf - 1 else jnp.where(mask, 0.0, f)
    for f in range(fields):
        fixed_ref[ks + nf + f] = air_ref[f, level_rows(0, tiles), :]

    def put(i, inv, out, back):
        fac[0, i] = inv
        fac[1, i] = out
        if back is not None:
            fac[2, i] = back

    middle = factor(lambda i: mix_ref[level_rows(i, tiles), :], depth, put)

    class Get:
        def __call__(self, i):
            return (fac[0, i], fac[1, i], fac[2, i])

    get = Get()
    for f in range(fields + 1):
        def rhs(i, f=f):
            if f < fields:
                return air_ref[f, level_rows(i, tiles), :]
            return jnp.ones_like(middle) if i == 0 else None

        def keep(i, v, f=f):
            work[f, i] = v

        def kept(i, f=f):
            return work[f, i]

        def store(i, v, f=f):
            x1[f, i] = v
            if f == fields:
                hg_ref[1, level_rows(i, tiles), :] = v

        apply_factor(rhs, depth, get, middle, keep, kept, store)
        top_ref[f] = x1[f, 0]
    for f in range(fields + 1):
        def rhs(i, f=f):
            return x1[f, i]

        def keep(i, v, f=f):
            work[f, i] = v

        def kept(i, f=f):
            return work[f, i]

        def store(i, v, f=f):
            if f < fields:
                y2_ref[f, level_rows(i, tiles), :] = v
            else:
                hg_ref[0, level_rows(i, tiles), :] = v

        apply_factor(rhs, depth, get, middle, keep, kept, store)


def first_bundle(cols, secs, cols_here, own_ref, m1_ref, m2_ref, src_ref, w_ref, out_ref):
    sec = lax.axis_index("sec")
    n = own_ref.shape[0]
    out_ref[0:n] = own_ref[...]
    out_ref[n : 2 * n] = m1_ref[...]
    out_ref[2 * n : 3 * n] = m2_ref[...]
    s = src_ref[...]
    band, within = split(s, cols_here * cols)
    owner, place = split(within, cols_here)
    code = (owner * 3 + section_slot(band, sec, secs)) * cols_here + place
    m = s.shape[0]
    out_ref[3 * n : 3 * n + m] = code.astype(jnp.float32)
    out_ref[3 * n + m : 3 * n + 2 * m] = w_ref[...]


def later_bundle(own_ref, m1_ref, m2_ref, out_ref):
    n = own_ref.shape[0]
    out_ref[0:n] = own_ref[...]
    out_ref[n : 2 * n] = m1_ref[...]
    out_ref[2 * n : 3 * n] = m2_ref[...]


def lane_gather(row, lane):
    return jnp.take_along_axis(jnp.broadcast_to(row, lane.shape), lane, axis=1)


def flux_kernel(later, pieces, cell_rows, *refs):
    tables, refs = refs[:pieces], refs[pieces:]
    code_ref, fixed_ref, refs = refs[0], refs[1], refs[2:]
    if later:
        top_ref, before_ref, refs = refs[0], refs[1], refs[2:]
    flux_ref, add_ref = refs
    ks = code_ref.shape[0]
    his, lanes, vals = [], [], []
    for k in range(ks):
        hi, lane = split(code_ref[k], LANES)
        his.append(hi)
        lanes.append(lane)
        vals.append([jnp.zeros(lane.shape, jnp.float32) for _ in range(2)])
    for slot in range(3):
        for j in range(pieces):
            for r in range(cell_rows):
                number = (slot * pieces + j) * cell_rows + r
                base = slot * 2 * cell_rows + r
                row0 = tables[j][base : base + 1, :]
                row1 = tables[j][base + cell_rows : base + cell_rows + 1, :]
                for k in range(ks):
                    hit = his[k] == number
                    vals[k][0] = jnp.where(hit, lane_gather(row0, lanes[k]), vals[k][0])
                    vals[k][1] = jnp.where(hit, lane_gather(row1, lanes[k]), vals[k][1])
    skin = fixed_ref[ks + 3]
    frozen = jnp.zeros_like(skin)
    for k in range(ks):
        skin = skin + fixed_ref[k] * vals[k][0]
        frozen = frozen + fixed_ref[k] * vals[k][1]
    bottom = [fixed_ref[ks + 4 + f] for f in range(4)]
    if later:
        g = top_ref[4]
        bottom = [top_ref[f] + g * before_ref[f] for f in range(4)]
    short, long_, rain = fixed_ref[ks], fixed_ref[ks + 1], fixed_ref[ks + 2]
    cover = 1.0 / (1.0 + frozen)
    speed = jnp.sqrt(bottom[2] * bottom[2] + bottom[3] * bottom[3] + 1.0)
    coefficient = 0.3 * speed * cover
    snow = 1.0 / (1.0 + jnp.exp(2.0 * skin))
    f0 = coefficient * (skin - bottom[0])
    f1 = coefficient * (0.5 * jnp.exp(0.3 * skin) - bottom[1])
    f2 = coefficient * bottom[2]
    f3 = coefficient * bottom[3]
    f4 = short * cover
    f5 = long_ - 0.2 * skin
    f6 = rain * (1.0 - snow)
    f7 = rain * snow
    n = skin.shape[0]
    for v, value in enumerate((f2, f3, f4 + f5 - f0 - f1, 0.4 * f1 - f6, f7)):
        flux_ref[v * n : (v + 1) * n] = value
    for v, value in enumerate((f0, f1, -f2, -f3)):
        add_ref[v] = value


def partial_kernel(pieces, cell_rows, offset, *refs):
    flux, refs = refs[:3], refs[3:]
    bundles, outs = refs[:pieces], refs[pieces:]
    col_rows = flux[0].shape[0] // FLUXES
    base = lax.axis_index("col") * (3 * col_rows)
    m = outs[0].shape[0] // FLUXES
    ks = (bundles[0].shape[0] - offset) // 2 // m
    per = SUBS // m
    for j in range(pieces):
        total = [None] * FLUXES
        for q in range(ks // per):
            code, w = [], []
            for k in range(q * per, (q + 1) * per):
                code.append(bundles[j][pl.ds(offset + k, m, stride=ks), :])
                w.append(bundles[j][pl.ds(offset + ks * m + k, m, stride=ks), :])
            code = jnp.concatenate(code, axis=0).astype(jnp.int32)
            w = jnp.concatenate(w, axis=0)
            hi, lane = split(code, LANES)
            hi = hi - base
            vals = [jnp.zeros(lane.shape, jnp.float32) for _ in range(FLUXES)]
            for slot in range(3):
                for r in range(col_rows):
                    hit = hi == slot * col_rows + r
                    for v in range(FLUXES):
                        row = flux[slot][v * col_rows + r : v * col_rows + r + 1, :]
                        vals[v] = jnp.where(hit, lane_gather(row, lane), vals[v])
            for v in range(FLUXES):
                part = w * vals[v]
                total[v] = part if total[v] is None else total[v] + part
        for v in range(FLUXES):
            whole = total[v][0:m]
            for p in range(1, per):
                whole = whole + total[v][p * m : (p + 1) * m]
            outs[j][v * m : (v + 1) * m] = whole


def sea_kernel(pieces, depth, last, *refs):
    parts, refs = refs[:pieces], refs[pieces:]
    state_ref, mix_ref, ice_ref, mask_ref, refs = refs[0], refs[1], refs[2], refs[3], refs[4:]
    out_ref, top_ref, fac, work = refs
    tiles = mix_ref.shape[0] // depth
    flux = []
    for v in range(FLUXES):
        total = parts[0][v * tiles : (v + 1) * tiles]
        for p in parts[1:]:
            total = total + p[v * tiles : (v + 1) * tiles]
        flux.append(total)
    ice = ice_ref[...]
    wet = mask_ref[...] == 1
    stress2 = 2.0 * jnp.sqrt(flux[0] * flux[0] + flux[1] * flux[1] + 0.01)
    heat, salt, snow = flux[2], flux[3], flux[4]
    open_water = 1.0 - ice
    adds = (0.5 * open_water * heat, 0.3 * open_water * salt)
    grown = ice / (ice + open_water * jnp.exp(0.5 * heat - 0.8 * snow))
    new_ice = jnp.where(wet, grown, ice)

    known = {}

    def mix(i):
        if i not in known:
            k = mix_ref[level_rows(i, tiles), :]
            known[i] = k * (1.0 + stress2 * math.exp(-i / 8.0))
        return known[i]

    def put(i, inv, out, back):
        fac[0, i] = inv
        fac[1, i] = out
        if back is not None:
            fac[2, i] = back

    middle = factor(mix, depth, put)
    for f in range(2):
        def rhs(i, f=f):
            r = state_ref[f, level_rows(i, tiles), :]
            return r + adds[f] if i == 0 else r

        def keep(i, v, f=f):
            work[f, i] = v

        def kept(i, f=f):
            return work[f, i]

        def store(i, v, f=f):
            new = jnp.where(wet, v, state_ref[f, level_rows(i, tiles), :])
            out_ref[f, level_rows(i, tiles), :] = new
            if f == 0 and i == 0 and not last:
                top_ref[0:tiles] = new

        apply_factor(rhs, depth, lambda i: (fac[0, i], fac[1, i], fac[2, i]), middle, keep, kept, store)
    if last:
        top_ref[...] = new_ice
    else:
        top_ref[tiles : 2 * tiles] = new_ice


def air_finish(y2_ref, hg_ref, first_ref, second_ref, out_ref):
    fields, tiles = first_ref.shape[0], first_ref.shape[1]
    rows = y2_ref.shape[1]
    for f in range(fields):
        for j in range(tiles):
            b1 = jnp.broadcast_to(first_ref[f, j : j + 1, :], (SUBS, LANES))
            b2 = jnp.broadcast_to(second_ref[f, j : j + 1, :], (SUBS, LANES))
            for t in range(rows // (SUBS * tiles)):
                at = slice((t * tiles + j) * SUBS, (t * tiles + j + 1) * SUBS)
                out_ref[f, at] = y2_ref[f, at] + hg_ref[0, at] * b1 + hg_ref[1, at] * b2


def call(kernel, name, out, *args, scratch=(), final=False):
    many = isinstance(out, list)
    kind = jax.ShapeDtypeStruct if final else pltpu.VMEM
    return pl.pallas_call(
        kernel,
        name=name,
        out_shape=[kind(*o) for o in out] if many else kind(*out),
        in_specs=[pl.BlockSpec(memory_space=pltpu.VMEM)] * len(args),
        out_specs=[pl.BlockSpec(memory_space=pltpu.VMEM)] * len(out) if many else pl.BlockSpec(memory_space=pltpu.VMEM),
        scratch_shapes=list(scratch),
        compiler_params=pltpu.CompilerParams(vmem_limit_bytes=8 << 20),
    )(*[pltpu.with_memory_space_constraint(a, pltpu.VMEM) for a in args])


def per_device(air_state, air_mix, surface_forcing, air_mask, ocean_sources, ocean_weights,
               sea_state, sea_mix, ice_cover, sea_mask, air_sources, air_weights):
    cols, secs = lax.axis_size("col"), lax.axis_size("sec")
    fields, levels, here = air_state.shape
    depth, cells = sea_mix.shape
    tiles, sea_tiles = here // LANES, cells // LANES
    f32, i32 = jnp.float32, jnp.int32
    ko = ocean_sources.shape[0]

    air = tile_rows(air_state)
    mixing = tile_rows(air_mix)
    sea = tile_rows(sea_state)
    sea_k = tile_rows(sea_mix)
    ice = ice_cover.reshape(sea_tiles, LANES)
    wet = sea_mask.reshape(sea_tiles, LANES)

    top = jnp.concatenate([sea_state[0, 0].reshape(sea_tiles, LANES), ice], axis=0)
    near = sec_exchange(top)
    y2, hg, tops, code, fixed = call(
        lambda *r: air_prepare(cols, secs, cells, *r), "air_prepare",
        [(air.shape, f32), ((2,) + mixing.shape, f32), ((fields + 1, tiles, LANES), f32),
         ((ko, tiles, LANES), i32), ((ko + 8, tiles, LANES), f32)],
        air, mixing, tile_rows(ocean_sources), tile_rows(ocean_weights), tile_rows(surface_forcing),
        air_mask.reshape(tiles, LANES),
        scratch=[pltpu.VMEM((3, levels, tiles, LANES), f32), pltpu.VMEM((fields + 1, levels, tiles, LANES), f32),
                 pltpu.VMEM((fields + 1, levels, tiles, LANES), f32)],
    )
    src, w = tile_rows(air_sources), tile_rows(air_weights)
    offset = 6 * sea_tiles
    bundle = call(
        lambda *r: first_bundle(cols, secs, here, *r), "first_bundle",
        ((offset + 2 * src.shape[0], LANES), f32), top, *near, src, w,
    )
    bundles = [bundle] + [lax.ppermute(bundle, "col", col_pairs(j)) for j in range(cols - 1, 0, -1)][::-1]
    adds, tables = [], bundles
    for step in range(STEPS):
        extra = (tops, adds[0]) if step else ()
        flux, add = call(
            lambda *r: flux_kernel(bool(step), cols, sea_tiles, *r), "fluxes",
            [((FLUXES * tiles, LANES), f32), ((fields, tiles, LANES), f32)],
            *tables, code, fixed, *extra,
        )
        adds.append(add)
        parts = call(
            lambda *r: partial_kernel(cols, sea_tiles, offset, *r), "partial_sums",
            [((FLUXES * sea_tiles, LANES), f32)] * cols,
            flux, *sec_exchange(flux), *bundles,
        )
        moved = [parts[0]] + [lax.ppermute(parts[j], "col", col_pairs(j)) for j in range(cols - 1, 0, -1)][::-1]
        last = step == STEPS - 1
        if last:
            air_out = call(air_finish, "air_finish", (air.shape, f32), y2, hg, *adds, final=True)
        sea, top = call(
            lambda *r: sea_kernel(cols, depth, last, *r), "sea_step",
            [(sea.shape, f32), ((sea_tiles if last else 2 * sea_tiles, LANES), f32)],
            *moved, sea, sea_k, ice, wet, final=last,
            scratch=[pltpu.VMEM((3, depth, sea_tiles, LANES), f32), pltpu.VMEM((2, depth, sea_tiles, LANES), f32)],
        )
        if not last:
            ice = top[sea_tiles:]
            bundle = call(later_bundle, "later_bundle", ((offset, LANES), f32), top, *sec_exchange(top))
            tables = [bundle] + [lax.ppermute(bundle, "col", col_pairs(j)) for j in range(cols - 1, 0, -1)][::-1]
    return (untile_rows(air_out, levels, here), untile_rows(sea, depth, cells), top.reshape(cells))


def solution(mesh):
    both = ("sec", "col")
    placed = (
        P(None, None, both), P(None, both), P(None, both), P(both), P(None, both), P(None, both),
        P(None, None, both), P(None, both), P(both), P(both), P(None, both), P(None, both),
    )
    return jax.shard_map(
        per_device,
        mesh=mesh,
        in_specs=placed,
        out_specs=(P(None, None, both), P(None, None, both), P(both)),
        check_vma=False,
    )
```

```python
import math

import jax
import jax.numpy as jnp
from jax import lax
from jax.experimental import pallas as pl
from jax.experimental.pallas import tpu as pltpu
from jax.sharding import PartitionSpec as P


STEPS = 2
LANES = 128
SUBS = 8
FLUXES = 5


def tile_rows(x):
    *lead, r, n = x.shape
    t = min(r, SUBS)
    y = x.reshape(*lead, r // t, t, n // LANES, LANES)
    return jnp.swapaxes(y, -3, -2).reshape(*lead, r * n // LANES, LANES)


def untile_rows(x, r, n):
    lead = x.shape[:-2]
    t = min(r, SUBS)
    y = x.reshape(*lead, r // t, n // LANES, t, LANES)
    return jnp.swapaxes(y, -3, -2).reshape(*lead, r, n)


def level_rows(level, tiles, height=SUBS):
    return pl.ds((level // height) * height * tiles + level % height, tiles, stride=height)


def split(x, size):
    if size & (size - 1) == 0:
        return x >> (size.bit_length() - 1), x & (size - 1)
    return x // size, x % size


def sec_partners():
    n = lax.axis_size("sec")
    if n % 2 == 0:
        return (
            [(i, i ^ 1) for i in range(n)],
            [(i, (i + 1) % n if i % 2 else (i - 1) % n) for i in range(n)],
        )
    return ([(i, (i + 1) % n) for i in range(n)], [(i, (i - 1) % n) for i in range(n)])


def section_slot(band, sec, n):
    odd = sec & 1 if n % 2 == 0 else 1
    return jnp.where(band == 1, 0, jnp.where((band == 0) == (odd == 1), 1, 2))


def col_pairs(j):
    n = lax.axis_size("col")
    if n & (n - 1) == 0:
        return [(i, i ^ j) for i in range(n)]
    return [(i, (i + j) % n) for i in range(n)]


def row_slot(owner, col, n):
    if n & (n - 1) == 0:
        return owner ^ col
    rest = col - owner
    return jnp.where(rest < 0, rest + n, rest)


def sec_exchange(x):
    return [lax.ppermute(x, "sec", pairs) for pairs in sec_partners()]


def col_exchange(pieces):
    got = [pieces[0]]
    for j in range(1, len(pieces)):
        got.append(lax.ppermute(pieces[j], "col", col_pairs(j)))
    return got


def factor(mix, depth, put):
    half = depth // 2
    one = jnp.ones_like(mix(0))
    sides = []
    for side in (0, 1):
        if side == 0:
            sides.append([one, one, None])
        else:
            sides.append([one + mix(depth - 1), one, None])
    scale = [None, None]
    last = [None, None]
    for step in range(half):
        for side in (0, 1):
            n, d, _ = sides[side]
            i = step if side == 0 else depth - 1 - step
            ahead = mix(i) if side == 0 else mix(i - 1)
            behind = None
            if step:
                behind = mix(i - 1) if side == 0 else mix(i)
            d1 = n + ahead * d
            r1 = 1.0 / d1
            inv = d * r1
            n1 = d1 + ahead * n
            if step % 4 == 3:
                d1, n1 = d1 * scale[side], n1 * scale[side]
            if step % 4 == 0:
                scale[side] = r1
            out = ahead * inv
            put(i, inv, out, None if behind is None else behind * inv)
            sides[side] = [n1, d1, None]
            last[side] = out
    return 1.0 / (1.0 - last[0] * last[1])


def apply_factor(rhs, depth, get, middle, keep, kept, store):
    half = depth // 2
    carry = [None, None]
    for step in range(half):
        for side in (0, 1):
            i = step if side == 0 else depth - 1 - step
            inv, _, back = get(i)
            r = rhs(i)
            value = None if r is None else r * inv
            if step and carry[side] is not None:
                moved = back * carry[side]
                value = moved if value is None else value + moved
            carry[side] = value
            if value is not None:
                keep(i, value)
    top, bottom = carry
    up, down = get(half - 1)[1], get(half)[1]
    x_top = (top if bottom is None else top + up * bottom) * middle
    x_bottom = down * x_top if bottom is None else bottom + down * x_top
    store(half - 1, x_top)
    store(half, x_bottom)
    xs = [x_top, x_bottom]
    for step in range(half - 2, -1, -1):
        for side in (0, 1):
            i = step if side == 0 else depth - 1 - step
            x = get(i)[1] * xs[side]
            if side == 0 or bottom is not None:
                x = x + kept(i)
            xs[side] = x
            store(i, x)


def fetch(pairs, sems):
    copies = [pltpu.make_async_copy(src, dst, sems.at[i]) for i, (src, dst) in enumerate(pairs)]
    for c in copies:
        c.start()
    return copies


def first_kernel(cols, secs, cells_here, cols_here,
                 sea_ref, ice_hbm, air_ref, src_hbm, w_hbm, forcing_hbm, mask_hbm, feed_hbm, feed_w_hbm, wet_hbm,
                 top_ref, code_ref, fixed_ref, feed_ref, ice_ref, wet_ref,
                 sea0, air0, src_ref, w_ref, forcing_ref, mask_ref, feed_in, feed_w, sems):
    tiles, sea_tiles = mask_ref.shape[0], ice_ref.shape[0]
    sec, col = lax.axis_index("sec"), lax.axis_index("col")
    copies = fetch(
        [(sea_ref.at[0, pl.ds(0, SUBS * sea_tiles)], sea0), (ice_hbm, ice_ref), (feed_hbm, feed_in), (feed_w_hbm, feed_w),
         (src_hbm, src_ref), (w_hbm, w_ref), (forcing_hbm, forcing_ref), (mask_hbm, mask_ref), (wet_hbm, wet_ref),
         (air_ref.at[:, pl.ds(0, SUBS * tiles)], air0)], sems)
    for c in copies:
        c.wait()
    top_ref[0:sea_tiles] = sea0[level_rows(0, sea_tiles), :]
    top_ref[sea_tiles:] = ice_ref[...]

    s = feed_in[...]
    band, within = split(s, cols_here * cols)
    owner, place = split(within, cols_here)
    code = (owner * 3 + section_slot(band, sec, secs)) * cols_here + place
    m = s.shape[0]
    feed_ref[0:m] = code.astype(jnp.float32)
    feed_ref[m : 2 * m] = feed_w[...]

    mask = mask_ref[...] == 1
    ks = src_ref.shape[0] // tiles
    for k in range(ks):
        s = src_ref[pl.ds(k, tiles, stride=ks), :]
        band, within = split(s, cells_here * cols)
        owner, place = split(within, cells_here)
        slot = section_slot(band, sec, secs) * cols + row_slot(owner, col, cols)
        code_ref[k] = slot * cells_here + place
        fixed_ref[k] = jnp.where(mask, w_ref[pl.ds(k, tiles, stride=ks), :], 0.0)
    nf = forcing_ref.shape[0] // tiles
    for k in range(nf):
        f = forcing_ref[pl.ds(k, tiles, stride=nf), :]
        fixed_ref[ks + k] = f if k < nf - 1 else jnp.where(mask, 0.0, f)
    for f in range(air0.shape[0]):
        fixed_ref[ks + nf + f] = air0[f, level_rows(0, tiles), :]


def air_prepare(air_hbm, mix_hbm, sea_hbm, sea_mix_hbm, y2_ref, hg_ref, top_ref, sea_ref, sea_mix_ref,
                air_ref, mix_ref, fac, work, x1, sems):
    depth = fac.shape[1]
    tiles = mix_ref.shape[0] // depth
    fields = air_ref.shape[0]
    copies = fetch(
        [(mix_hbm, mix_ref)] + [(air_hbm.at[f], air_ref.at[f]) for f in range(fields)]
        + [(sea_hbm, sea_ref), (sea_mix_hbm, sea_mix_ref)], sems)
    copies[0].wait()

    def put(i, inv, out, back):
        fac[0, i] = inv
        fac[1, i] = out
        if back is not None:
            fac[2, i] = back

    middle = factor(lambda i: mix_ref[level_rows(i, tiles), :], depth, put)

    class Get:
        def __call__(self, i):
            return (fac[0, i], fac[1, i], fac[2, i])

    get = Get()
    for f in [fields] + list(range(fields)):
        if f < fields:
            copies[1 + f].wait()

        def rhs(i, f=f):
            if f < fields:
                return air_ref[f, level_rows(i, tiles), :]
            return jnp.ones_like(middle) if i == 0 else None

        def keep(i, v, f=f):
            work[f, i] = v

        def kept(i, f=f):
            return work[f, i]

        def store(i, v, f=f):
            x1[f, i] = v
            if f == fields:
                hg_ref[1, level_rows(i, tiles), :] = v

        apply_factor(rhs, depth, get, middle, keep, kept, store)
        top_ref[f] = x1[f, 0]
    for f in range(fields + 1):
        def rhs(i, f=f):
            return x1[f, i]

        def keep(i, v, f=f):
            work[f, i] = v

        def kept(i, f=f):
            return work[f, i]

        def store(i, v, f=f):
            if f < fields:
                y2_ref[f, level_rows(i, tiles), :] = v
            else:
                hg_ref[0, level_rows(i, tiles), :] = v

        apply_factor(rhs, depth, get, middle, keep, kept, store)
    for c in copies[1 + fields :]:
        c.wait()


def first_bundle(own_ref, m1_ref, m2_ref, feed_ref, out_ref):
    n = own_ref.shape[0]
    later_bundle(own_ref, m1_ref, m2_ref, out_ref.at[0 : 3 * n])
    out_ref[3 * n :] = feed_ref[...]


def later_bundle(own_ref, m1_ref, m2_ref, out_ref):
    n = own_ref.shape[0]
    out_ref[0:n] = own_ref[...]
    out_ref[n : 2 * n] = m1_ref[...]
    out_ref[2 * n : 3 * n] = m2_ref[...]


def lane_gather(row, lane):
    return jnp.take_along_axis(jnp.broadcast_to(row, lane.shape), lane, axis=1)


def flux_kernel(later, pieces, cell_rows, *refs):
    tables, refs = refs[:pieces], refs[pieces:]
    code_ref, fixed_ref, refs = refs[0], refs[1], refs[2:]
    if later:
        top_ref, before_ref, refs = refs[0], refs[1], refs[2:]
    flux_ref, add_ref = refs
    ks = code_ref.shape[0]
    his, lanes, vals = [], [], []
    for k in range(ks):
        hi, lane = split(code_ref[k], LANES)
        his.append(hi)
        lanes.append(lane)
        vals.append([jnp.zeros(lane.shape, jnp.float32) for _ in range(2)])
    for slot in range(3):
        for j in range(pieces):
            for r in range(cell_rows):
                number = (slot * pieces + j) * cell_rows + r
                base = slot * 2 * cell_rows + r
                row0 = tables[j][base : base + 1, :]
                row1 = tables[j][base + cell_rows : base + cell_rows + 1, :]
                for k in range(ks):
                    hit = his[k] == number
                    vals[k][0] = jnp.where(hit, lane_gather(row0, lanes[k]), vals[k][0])
                    vals[k][1] = jnp.where(hit, lane_gather(row1, lanes[k]), vals[k][1])
    skin = fixed_ref[ks + 3]
    frozen = jnp.zeros_like(skin)
    for k in range(ks):
        skin = skin + fixed_ref[k] * vals[k][0]
        frozen = frozen + fixed_ref[k] * vals[k][1]
    bottom = [fixed_ref[ks + 4 + f] for f in range(4)]
    if later:
        g = top_ref[4]
        bottom = [top_ref[f] + g * before_ref[f] for f in range(4)]
    short, long_, rain = fixed_ref[ks], fixed_ref[ks + 1], fixed_ref[ks + 2]
    cover = 1.0 / (1.0 + frozen)
    speed = jnp.sqrt(bottom[2] * bottom[2] + bottom[3] * bottom[3] + 1.0)
    coefficient = 0.3 * speed * cover
    snow = 1.0 / (1.0 + jnp.exp(2.0 * skin))
    f0 = coefficient * (skin - bottom[0])
    f1 = coefficient * (0.5 * jnp.exp(0.3 * skin) - bottom[1])
    f2 = coefficient * bottom[2]
    f3 = coefficient * bottom[3]
    f4 = short * cover
    f5 = long_ - 0.2 * skin
    f6 = rain * (1.0 - snow)
    f7 = rain * snow
    n = skin.shape[0]
    for v, value in enumerate((f2, f3, f4 + f5 - f0 - f1, 0.4 * f1 - f6, f7)):
        flux_ref[v * n : (v + 1) * n] = value
    for v, value in enumerate((f0, f1, -f2, -f3)):
        add_ref[v] = value


def partial_kernel(pieces, offset, *refs):
    flux, refs = refs[:3], refs[3:]
    bundles, outs = refs[:pieces], refs[pieces:]
    col_rows = flux[0].shape[0] // FLUXES
    base = lax.axis_index("col") * (3 * col_rows)
    m = outs[0].shape[0] // FLUXES
    ks = (bundles[0].shape[0] - offset) // 2 // m
    per = SUBS // m
    for j in range(pieces):
        total = [None] * FLUXES
        for q in range(ks // per):
            code, w = [], []
            for k in range(q * per, (q + 1) * per):
                code.append(bundles[j][pl.ds(offset + k, m, stride=ks), :])
                w.append(bundles[j][pl.ds(offset + ks * m + k, m, stride=ks), :])
            code = jnp.concatenate(code, axis=0).astype(jnp.int32)
            w = jnp.concatenate(w, axis=0)
            hi, lane = split(code, LANES)
            hi = hi - base
            vals = [jnp.zeros(lane.shape, jnp.float32) for _ in range(FLUXES)]
            for slot in range(3):
                for r in range(col_rows):
                    hit = hi == slot * col_rows + r
                    for v in range(FLUXES):
                        row = flux[slot][v * col_rows + r : v * col_rows + r + 1, :]
                        vals[v] = jnp.where(hit, lane_gather(row, lane), vals[v])
            for v in range(FLUXES):
                part = w * vals[v]
                total[v] = part if total[v] is None else total[v] + part
        for v in range(FLUXES):
            whole = total[v][0:m]
            for p in range(1, per):
                whole = whole + total[v][p * m : (p + 1) * m]
            outs[j][v * m : (v + 1) * m] = whole


def sea_kernel(pieces, depth, last, *refs):
    parts, refs = refs[:pieces], refs[pieces:]
    state_ref, mix_ref, ice_ref, mask_ref, refs = refs[0], refs[1], refs[2], refs[3], refs[4:]
    out_ref, top_ref, fac, work = refs
    tiles = mix_ref.shape[0] // depth
    flux = []
    for v in range(FLUXES):
        total = parts[0][v * tiles : (v + 1) * tiles]
        for p in parts[1:]:
            total = total + p[v * tiles : (v + 1) * tiles]
        flux.append(total)
    ice = ice_ref[...]
    wet = mask_ref[...] == 1
    stress2 = 2.0 * jnp.sqrt(flux[0] * flux[0] + flux[1] * flux[1] + 0.01)
    heat, salt, snow = flux[2], flux[3], flux[4]
    open_water = 1.0 - ice
    adds = (0.5 * open_water * heat, 0.3 * open_water * salt)
    grown = ice / (ice + open_water * jnp.exp(0.5 * heat - 0.8 * snow))
    new_ice = jnp.where(wet, grown, ice)

    known = {}

    def mix(i):
        if i not in known:
            k = mix_ref[level_rows(i, tiles), :]
            known[i] = k * (1.0 + stress2 * math.exp(-i / 8.0))
        return known[i]

    def put(i, inv, out, back):
        fac[0, i] = inv
        fac[1, i] = out
        if back is not None:
            fac[2, i] = back

    middle = factor(mix, depth, put)
    for f in range(2):
        def rhs(i, f=f):
            r = state_ref[f, level_rows(i, tiles), :]
            return r + adds[f] if i == 0 else r

        def keep(i, v, f=f):
            work[f, i] = v

        def kept(i, f=f):
            return work[f, i]

        def store(i, v, f=f):
            new = jnp.where(wet, v, state_ref[f, level_rows(i, tiles), :])
            out_ref[f, level_rows(i, tiles), :] = new
            if f == 0 and i == 0 and not last:
                top_ref[0:tiles] = new

        apply_factor(rhs, depth, lambda i: (fac[0, i], fac[1, i], fac[2, i]), middle, keep, kept, store)
    if last:
        top_ref[...] = new_ice
    else:
        top_ref[tiles : 2 * tiles] = new_ice


def air_finish(y2_ref, hg_ref, first_ref, second_ref, out_ref):
    fields, tiles = first_ref.shape[0], first_ref.shape[1]
    rows = y2_ref.shape[1]
    for f in range(fields):
        for j in range(tiles):
            b1 = jnp.broadcast_to(first_ref[f, j : j + 1, :], (SUBS, LANES))
            b2 = jnp.broadcast_to(second_ref[f, j : j + 1, :], (SUBS, LANES))
            for t in range(rows // (SUBS * tiles)):
                at = slice((t * tiles + j) * SUBS, (t * tiles + j + 1) * SUBS)
                out_ref[f, at] = y2_ref[f, at] + hg_ref[0, at] * b1 + hg_ref[1, at] * b2


def call(kernel, out, *args, scratch=(), final=False, raw=False):
    many = isinstance(out, list)
    kind = jax.ShapeDtypeStruct if final else pltpu.VMEM
    return pl.pallas_call(
        kernel,
        out_shape=[kind(*o) for o in out] if many else kind(*out),
        in_specs=[pl.BlockSpec(memory_space=pltpu.HBM if raw else pltpu.VMEM)] * len(args),
        out_specs=[pl.BlockSpec(memory_space=pltpu.VMEM)] * len(out) if many else pl.BlockSpec(memory_space=pltpu.VMEM),
        scratch_shapes=list(scratch),
        compiler_params=pltpu.CompilerParams(vmem_limit_bytes=8 << 20),
    )(*[pltpu.with_memory_space_constraint(a, pltpu.HBM if raw else pltpu.VMEM) for a in args])


def per_device(air_state, air_mix, surface_forcing, air_mask, ocean_sources, ocean_weights,
               sea_state, sea_mix, ice_cover, sea_mask, air_sources, air_weights):
    cols, secs = lax.axis_size("col"), lax.axis_size("sec")
    fields, levels, here = air_state.shape
    depth, cells = sea_mix.shape
    tiles, sea_tiles = here // LANES, cells // LANES
    f32, i32 = jnp.float32, jnp.int32
    ko = ocean_sources.shape[0]

    air = tile_rows(air_state)
    mixing = tile_rows(air_mix)
    sea = tile_rows(sea_state)
    sea_k = tile_rows(sea_mix)
    ice = ice_cover.reshape(sea_tiles, LANES)
    wet = sea_mask.reshape(sea_tiles, LANES)

    offset = 6 * sea_tiles
    feed_rows = 2 * air_sources.shape[0] * sea_tiles
    smalls = [tile_rows(v) for v in (ocean_sources, ocean_weights, surface_forcing)]
    feeds = [tile_rows(v) for v in (air_sources, air_weights)]
    top, code, fixed, feed, ice, wet = call(
        lambda *r: first_kernel(cols, secs, cells, here, *r),
        [((2 * sea_tiles, LANES), f32), ((ko, tiles, LANES), i32), ((ko + 8, tiles, LANES), f32),
         ((feed_rows, LANES), f32), (ice.shape, f32), (wet.shape, i32)],
        sea, ice, air, *smalls, air_mask.reshape(tiles, LANES), *feeds, wet, raw=True,
        scratch=[pltpu.VMEM((SUBS * sea_tiles, LANES), f32), pltpu.VMEM((fields, SUBS * tiles, LANES), f32),
                 *[pltpu.VMEM(v.shape, v.dtype) for v in smalls], pltpu.VMEM((tiles, LANES), i32),
                 *[pltpu.VMEM(v.shape, v.dtype) for v in feeds], pltpu.SemaphoreType.DMA((10,))],
    )
    near = sec_exchange(top)
    bundle = call(first_bundle, ((offset + feed_rows, LANES), f32), top, *near, feed)
    y2, hg, tops, sea, sea_k = call(
        air_prepare,
        [(air.shape, f32), ((2,) + mixing.shape, f32), ((fields + 1, tiles, LANES), f32), (sea.shape, f32), (sea_k.shape, f32)],
        air, mixing, sea, sea_k, raw=True,
        scratch=[pltpu.VMEM(air.shape, f32), pltpu.VMEM(mixing.shape, f32), pltpu.VMEM((3, levels, tiles, LANES), f32),
                 pltpu.VMEM((fields + 1, levels, tiles, LANES), f32), pltpu.VMEM((fields + 1, levels, tiles, LANES), f32),
                 pltpu.SemaphoreType.DMA((fields + 3,))],
    )
    bundles = col_exchange([bundle] * cols)
    adds, tables = [], bundles
    for step in range(STEPS):
        extra = (tops, adds[0]) if step else ()
        flux, add = call(
            lambda *r: flux_kernel(bool(step), cols, sea_tiles, *r),
            [((FLUXES * tiles, LANES), f32), ((fields, tiles, LANES), f32)],
            *tables, code, fixed, *extra,
        )
        adds.append(add)
        parts = call(
            lambda *r: partial_kernel(cols, offset, *r),
            [((FLUXES * sea_tiles, LANES), f32)] * cols,
            flux, *sec_exchange(flux), *bundles,
        )
        moved = col_exchange(parts)
        last = step == STEPS - 1
        if last:
            air_out = call(air_finish, (air.shape, f32), y2, hg, *adds, final=True)
        sea, top = call(
            lambda *r: sea_kernel(cols, depth, last, *r),
            [(sea.shape, f32), ((sea_tiles if last else 2 * sea_tiles, LANES), f32)],
            *moved, sea, sea_k, ice, wet, final=last,
            scratch=[pltpu.VMEM((3, depth, sea_tiles, LANES), f32), pltpu.VMEM((2, depth, sea_tiles, LANES), f32)],
        )
        if not last:
            ice = top[sea_tiles:]
            bundle = call(later_bundle, ((offset, LANES), f32), top, *sec_exchange(top))
            tables = col_exchange([bundle] * cols)
    return (untile_rows(air_out, levels, here), untile_rows(sea, depth, cells), top.reshape(cells))


def solution(mesh):
    both = ("sec", "col")
    placed = (
        P(None, None, both), P(None, both), P(None, both), P(both), P(None, both), P(None, both),
        P(None, None, both), P(None, both), P(both), P(both), P(None, both), P(None, both),
    )
    return jax.shard_map(
        per_device,
        mesh=mesh,
        in_specs=placed,
        out_specs=(P(None, None, both), P(None, None, both), P(both)),
        check_vma=False,
    )
```

```python
import math

import jax
import jax.numpy as jnp
from jax import lax
from jax.experimental import pallas as pl
from jax.experimental.pallas import tpu as pltpu
from jax.sharding import PartitionSpec as P


STEPS = 2
LANES = 128
SUBS = 8
FLUXES = 5


def tile_rows(x):
    *lead, r, n = x.shape
    t = min(r, SUBS)
    y = x.reshape(*lead, r // t, t, n // LANES, LANES)
    return jnp.swapaxes(y, -3, -2).reshape(*lead, r * n // LANES, LANES)


def untile_rows(x, r, n):
    lead = x.shape[:-2]
    t = min(r, SUBS)
    y = x.reshape(*lead, r // t, n // LANES, t, LANES)
    return jnp.swapaxes(y, -3, -2).reshape(*lead, r, n)


def level_rows(level, tiles, height=SUBS):
    return pl.ds((level // height) * height * tiles + level % height, tiles, stride=height)


def split(x, size):
    if size & (size - 1) == 0:
        return x >> (size.bit_length() - 1), x & (size - 1)
    return x // size, x % size


def sec_partners():
    n = lax.axis_size("sec")
    if n % 2 == 0:
        return (
            [(i, i ^ 1) for i in range(n)],
            [(i, (i + 1) % n if i % 2 else (i - 1) % n) for i in range(n)],
        )
    return ([(i, (i + 1) % n) for i in range(n)], [(i, (i - 1) % n) for i in range(n)])


def section_slot(band, sec, n):
    odd = sec & 1 if n % 2 == 0 else 1
    return jnp.where(band == 1, 0, jnp.where((band == 0) == (odd == 1), 1, 2))


def col_pairs(j):
    n = lax.axis_size("col")
    if n & (n - 1) == 0:
        return [(i, i ^ j) for i in range(n)]
    return [(i, (i + j) % n) for i in range(n)]


def row_slot(owner, col, n):
    if n & (n - 1) == 0:
        return owner ^ col
    rest = col - owner
    return jnp.where(rest < 0, rest + n, rest)


def sec_exchange(x):
    got = []
    for pairs in sec_partners():
        got.append(lax.ppermute(x, "sec", pairs))
    return got


def col_exchange(pieces):
    got = [pieces[0]]
    for j in range(1, len(pieces)):
        got.append(lax.ppermute(pieces[j], "col", col_pairs(j)))
    return got


def factor(mix, depth, put):
    half = depth // 2
    one = jnp.ones_like(mix(0))
    sides = []
    for side in (0, 1):
        if side == 0:
            sides.append([one, one, None])
        else:
            sides.append([one + mix(depth - 1), one, None])
    scale = [None, None]
    last = [None, None]
    for step in range(half):
        for side in (0, 1):
            n, d, _ = sides[side]
            i = step if side == 0 else depth - 1 - step
            ahead = mix(i) if side == 0 else mix(i - 1)
            behind = None
            if step:
                behind = mix(i - 1) if side == 0 else mix(i)
            d1 = n + ahead * d
            r1 = 1.0 / d1
            inv = d * r1
            n1 = d1 + ahead * n
            if step % 4 == 3:
                d1, n1 = d1 * scale[side], n1 * scale[side]
            if step % 4 == 0:
                scale[side] = r1
            out = ahead * inv
            put(i, inv, out, None if behind is None else behind * inv)
            sides[side] = [n1, d1, None]
            last[side] = out
    return 1.0 / (1.0 - last[0] * last[1])


def apply_factor(rhs, depth, get, middle, keep, kept, store):
    half = depth // 2
    carry = [None, None]
    for step in range(half):
        for side in (0, 1):
            i = step if side == 0 else depth - 1 - step
            inv, _, back = get(i)
            r = rhs(i)
            value = None if r is None else r * inv
            if step and carry[side] is not None:
                moved = back * carry[side]
                value = moved if value is None else value + moved
            carry[side] = value
            if value is not None:
                keep(i, value)
    top, bottom = carry
    up, down = get(half - 1)[1], get(half)[1]
    x_top = (top if bottom is None else top + up * bottom) * middle
    x_bottom = down * x_top if bottom is None else bottom + down * x_top
    store(half - 1, x_top)
    store(half, x_bottom)
    xs = [x_top, x_bottom]
    for step in range(half - 2, -1, -1):
        for side in (0, 1):
            i = step if side == 0 else depth - 1 - step
            x = get(i)[1] * xs[side]
            if side == 0 or bottom is not None:
                x = x + kept(i)
            xs[side] = x
            store(i, x)


def fetch(pairs, sems):
    copies = [pltpu.make_async_copy(src, dst, sems.at[i]) for i, (src, dst) in enumerate(pairs)]
    for c in copies:
        c.start()
    return copies


def first_top(sea_hbm, ice_hbm, top_ref, sea0, sems):
    n = ice_hbm.shape[0]
    copies = fetch([(sea_hbm.at[0, pl.ds(0, SUBS * n)], sea0), (ice_hbm, top_ref.at[pl.ds(n, n)])], sems)
    for c in copies:
        c.wait()
    top_ref[0:n] = sea0[level_rows(0, n), :]


def first_rest(cols, secs, cells_here, cols_here,
               air_hbm, src_hbm, w_hbm, forcing_hbm, mask_hbm, feed_hbm, feed_w_hbm, wet_hbm,
               code_ref, fixed_ref, feed_ref, wet_ref,
               air0, src_ref, w_ref, forcing_ref, mask_ref, feed_in, sems):
    tiles = mask_ref.shape[0]
    m = feed_in.shape[0]
    sec, col = lax.axis_index("sec"), lax.axis_index("col")
    copies = fetch(
        [(feed_hbm, feed_in), (feed_w_hbm, feed_ref.at[pl.ds(m, m)]),
         (src_hbm, src_ref), (w_hbm, w_ref), (forcing_hbm, forcing_ref), (mask_hbm, mask_ref), (wet_hbm, wet_ref),
         (air_hbm.at[:, pl.ds(0, SUBS * tiles)], air0)], sems)
    for c in copies:
        c.wait()
    band, within = split(feed_in[...], cols_here * cols)
    owner, place = split(within, cols_here)
    code = (owner * 3 + section_slot(band, sec, secs)) * cols_here + place
    feed_ref[0:m] = code.astype(jnp.float32)

    mask = mask_ref[...] == 1
    ks = src_ref.shape[0] // tiles
    for k in range(ks):
        s = src_ref[pl.ds(k, tiles, stride=ks), :]
        band, within = split(s, cells_here * cols)
        owner, place = split(within, cells_here)
        slot = section_slot(band, sec, secs) * cols + row_slot(owner, col, cols)
        code_ref[k] = slot * cells_here + place
        fixed_ref[k] = jnp.where(mask, w_ref[pl.ds(k, tiles, stride=ks), :], 0.0)
    nf = forcing_ref.shape[0] // tiles
    for k in range(nf):
        f = forcing_ref[pl.ds(k, tiles, stride=nf), :]
        fixed_ref[ks + k] = f if k < nf - 1 else jnp.where(mask, 0.0, f)
    for f in range(air0.shape[0]):
        fixed_ref[ks + nf + f] = air0[f, level_rows(0, tiles), :]


def air_prepare(air_hbm, mix_hbm, sea_hbm, sea_mix_hbm, y2_ref, hg_ref, top_ref, sea_ref, sea_mix_ref,
                air_ref, mix_ref, fac, work, x1, sems):
    depth = fac.shape[1]
    tiles = mix_ref.shape[0] // depth
    fields = air_ref.shape[0]
    copies = fetch(
        [(mix_hbm, mix_ref)] + [(air_hbm.at[f], air_ref.at[f]) for f in range(fields)]
        + [(sea_hbm, sea_ref), (sea_mix_hbm, sea_mix_ref)], sems)
    copies[0].wait()

    def put(i, inv, out, back):
        fac[0, i] = inv
        fac[1, i] = out
        if back is not None:
            fac[2, i] = back

    middle = factor(lambda i: mix_ref[level_rows(i, tiles), :], depth, put)

    class Get:
        def __call__(self, i):
            return (fac[0, i], fac[1, i], fac[2, i])

    get = Get()
    for f in [fields] + list(range(fields)):
        if f < fields:
            copies[1 + f].wait()

        def rhs(i, f=f):
            if f < fields:
                return air_ref[f, level_rows(i, tiles), :]
            return jnp.ones_like(middle) if i == 0 else None

        def keep(i, v, f=f):
            work[f, i] = v

        def kept(i, f=f):
            return work[f, i]

        def store(i, v, f=f):
            x1[f, i] = v
            if f == fields:
                hg_ref[1, level_rows(i, tiles), :] = v

        apply_factor(rhs, depth, get, middle, keep, kept, store)
        top_ref[f] = x1[f, 0]
    for f in range(fields + 1):
        def rhs(i, f=f):
            return x1[f, i]

        def keep(i, v, f=f):
            work[f, i] = v

        def kept(i, f=f):
            return work[f, i]

        def store(i, v, f=f):
            if f < fields:
                y2_ref[f, level_rows(i, tiles), :] = v
            else:
                hg_ref[0, level_rows(i, tiles), :] = v

        apply_factor(rhs, depth, get, middle, keep, kept, store)
    for c in copies[1 + fields :]:
        c.wait()


def first_bundle(own_ref, m1_ref, m2_ref, feed_ref, out_ref):
    n = own_ref.shape[0]
    later_bundle(own_ref, m1_ref, m2_ref, out_ref.at[0 : 3 * n])
    out_ref[3 * n :] = feed_ref[...]


def later_bundle(own_ref, m1_ref, m2_ref, out_ref):
    n = own_ref.shape[0]
    out_ref[0:n] = own_ref[...]
    out_ref[n : 2 * n] = m1_ref[...]
    out_ref[2 * n : 3 * n] = m2_ref[...]


def lane_gather(row, lane):
    return jnp.take_along_axis(jnp.broadcast_to(row, lane.shape), lane, axis=1)


def flux_kernel(later, pieces, cell_rows, *refs):
    tables, refs = refs[:pieces], refs[pieces:]
    code_ref, fixed_ref, refs = refs[0], refs[1], refs[2:]
    if later:
        top_ref, before_ref, refs = refs[0], refs[1], refs[2:]
    flux_ref, add_ref = refs
    ks = code_ref.shape[0]
    his, lanes, vals = [], [], []
    for k in range(ks):
        hi, lane = split(code_ref[k], LANES)
        his.append(hi)
        lanes.append(lane)
        vals.append([jnp.zeros(lane.shape, jnp.float32) for _ in range(2)])
    for k in range(ks):
        for slot in range(3):
            for j in range(pieces):
                for r in range(cell_rows):
                    hit = his[k] == (slot * pieces + j) * cell_rows + r
                    base = slot * 2 * cell_rows + r
                    for v in range(2):
                        at = base + v * cell_rows
                        found = lane_gather(tables[j][at : at + 1, :], lanes[k])
                        vals[k][v] = jnp.where(hit, found, vals[k][v])
    skin = fixed_ref[ks + 3]
    frozen = jnp.zeros_like(skin)
    for k in range(ks):
        skin = skin + fixed_ref[k] * vals[k][0]
        frozen = frozen + fixed_ref[k] * vals[k][1]
    bottom = [fixed_ref[ks + 4 + f] for f in range(4)]
    if later:
        g = top_ref[4]
        bottom = [top_ref[f] + g * before_ref[f] for f in range(4)]
    short, long_, rain = fixed_ref[ks], fixed_ref[ks + 1], fixed_ref[ks + 2]
    cover = 1.0 / (1.0 + frozen)
    speed = jnp.sqrt(bottom[2] * bottom[2] + bottom[3] * bottom[3] + 1.0)
    coefficient = 0.3 * speed * cover
    snow = 1.0 / (1.0 + jnp.exp(2.0 * skin))
    f0 = coefficient * (skin - bottom[0])
    f1 = coefficient * (0.5 * jnp.exp(0.3 * skin) - bottom[1])
    f2 = coefficient * bottom[2]
    f3 = coefficient * bottom[3]
    f4 = short * cover
    f5 = long_ - 0.2 * skin
    f6 = rain * (1.0 - snow)
    f7 = rain * snow
    n = skin.shape[0]
    for v, value in enumerate((f2, f3, f4 + f5 - f0 - f1, 0.4 * f1 - f6, f7)):
        flux_ref[v * n : (v + 1) * n] = value
    for v, value in enumerate((f0, f1, -f2, -f3)):
        add_ref[v] = value


def partial_kernel(offset, slots, pieces, *refs):
    flux, refs = refs[: len(slots)], refs[len(slots) :]
    bundles, refs = refs[:pieces], refs[pieces:]
    before, outs = refs[:-pieces], refs[-pieces:]
    col_rows = flux[0].shape[0] // FLUXES
    base = lax.axis_index("col") * (3 * col_rows)
    m = outs[0].shape[0] // FLUXES
    ks = (bundles[0].shape[0] - offset) // 2 // m
    per = SUBS // m
    for j in range(pieces):
        total = [None] * FLUXES
        for q in range(ks // per):
            code, w = [], []
            for k in range(q * per, (q + 1) * per):
                code.append(bundles[j][pl.ds(offset + k, m, stride=ks), :])
                w.append(bundles[j][pl.ds(offset + ks * m + k, m, stride=ks), :])
            code = jnp.concatenate(code, axis=0).astype(jnp.int32)
            w = jnp.concatenate(w, axis=0)
            hi, lane = split(code, LANES)
            hi = hi - base
            vals = [jnp.zeros(lane.shape, jnp.float32) for _ in range(FLUXES)]
            for table, slot in zip(flux, slots):
                for r in range(col_rows):
                    hit = hi == slot * col_rows + r
                    for v in range(FLUXES):
                        row = table[v * col_rows + r : v * col_rows + r + 1, :]
                        vals[v] = jnp.where(hit, lane_gather(row, lane), vals[v])
            for v in range(FLUXES):
                part = w * vals[v]
                total[v] = part if total[v] is None else total[v] + part
        for v in range(FLUXES):
            at = slice(v * m, (v + 1) * m)
            whole = total[v][0:m]
            for p in range(1, per):
                whole = whole + total[v][p * m : (p + 1) * m]
            outs[j][at] = whole + before[j][at] if before else whole


def sea_kernel(pieces, depth, last, *refs):
    parts, refs = refs[:pieces], refs[pieces:]
    state_ref, mix_ref, ice_ref, mask_ref, refs = refs[0], refs[1], refs[2], refs[3], refs[4:]
    if last:
        out_hbm, top_hbm, fac, work, out_ref, top_ref, sems = refs
    else:
        out_ref, top_ref, fac, work = refs
    tiles = mix_ref.shape[0] // depth
    flux = []
    for v in range(FLUXES):
        total = parts[0][v * tiles : (v + 1) * tiles]
        for p in parts[1:]:
            total = total + p[v * tiles : (v + 1) * tiles]
        flux.append(total)
    ice = ice_ref[...]
    wet = mask_ref[...] == 1
    stress2 = 2.0 * jnp.sqrt(flux[0] * flux[0] + flux[1] * flux[1] + 0.01)
    heat, salt, snow = flux[2], flux[3], flux[4]
    open_water = 1.0 - ice
    adds = (0.5 * open_water * heat, 0.3 * open_water * salt)
    grown = ice / (ice + open_water * jnp.exp(0.5 * heat - 0.8 * snow))
    new_ice = jnp.where(wet, grown, ice)

    known = {}

    def mix(i):
        if i not in known:
            k = mix_ref[level_rows(i, tiles), :]
            known[i] = k * (1.0 + stress2 * math.exp(-i / 8.0))
        return known[i]

    def put(i, inv, out, back):
        fac[0, i] = inv
        fac[1, i] = out
        if back is not None:
            fac[2, i] = back

    copies = []
    if last:
        top_ref[...] = new_ice
        copies.append(pltpu.make_async_copy(top_ref, top_hbm, sems.at[2]))
        copies[-1].start()
    else:
        top_ref[tiles : 2 * tiles] = new_ice
    middle = factor(mix, depth, put)
    for f in range(2):
        def rhs(i, f=f):
            r = state_ref[f, level_rows(i, tiles), :]
            return r + adds[f] if i == 0 else r

        def keep(i, v, f=f):
            work[f, i] = v

        def kept(i, f=f):
            return work[f, i]

        def store(i, v, f=f):
            new = jnp.where(wet, v, state_ref[f, level_rows(i, tiles), :])
            out_ref[f, level_rows(i, tiles), :] = new
            if f == 0 and i == 0 and not last:
                top_ref[0:tiles] = new

        apply_factor(rhs, depth, lambda i: (fac[0, i], fac[1, i], fac[2, i]), middle, keep, kept, store)
        if last:
            copies.append(pltpu.make_async_copy(out_ref.at[f], out_hbm.at[f], sems.at[f]))
            copies[-1].start()
    for c in copies:
        c.wait()


def air_finish(y2_ref, hg_ref, first_ref, second_ref, out_ref):
    fields, tiles = first_ref.shape[0], first_ref.shape[1]
    rows = y2_ref.shape[1]
    for f in range(fields):
        for j in range(tiles):
            b1 = jnp.broadcast_to(first_ref[f, j : j + 1, :], (SUBS, LANES))
            b2 = jnp.broadcast_to(second_ref[f, j : j + 1, :], (SUBS, LANES))
            for t in range(rows // (SUBS * tiles)):
                at = slice((t * tiles + j) * SUBS, (t * tiles + j + 1) * SUBS)
                out_ref[f, at] = y2_ref[f, at] + hg_ref[0, at] * b1 + hg_ref[1, at] * b2


def call(kernel, out, *args, scratch=(), out_space=pltpu.VMEM, space=pltpu.VMEM):
    spaces = out_space if isinstance(out_space, list) else [out_space] * len(out)
    return pl.pallas_call(
        kernel,
        out_shape=[pltpu.VMEM(*o) if sp is pltpu.VMEM else jax.ShapeDtypeStruct(*o) for o, sp in zip(out, spaces)],
        in_specs=[pl.BlockSpec(memory_space=space)] * len(args),
        out_specs=[pl.BlockSpec(memory_space=sp or pltpu.VMEM) for sp in spaces],
        scratch_shapes=list(scratch),
        compiler_params=pltpu.CompilerParams(vmem_limit_bytes=8 << 20),
    )(*[pltpu.with_memory_space_constraint(a, space) for a in args])


def per_device(air_state, air_mix, surface_forcing, air_mask, ocean_sources, ocean_weights,
               sea_state, sea_mix, ice_cover, sea_mask, air_sources, air_weights):
    cols, secs = lax.axis_size("col"), lax.axis_size("sec")
    fields, levels, here = air_state.shape
    depth, cells = sea_mix.shape
    tiles, sea_tiles = here // LANES, cells // LANES
    f32, i32 = jnp.float32, jnp.int32
    ko = ocean_sources.shape[0]

    air = tile_rows(air_state)
    mixing = tile_rows(air_mix)
    sea = tile_rows(sea_state)
    sea_k = tile_rows(sea_mix)
    ice = ice_cover.reshape(sea_tiles, LANES)
    wet = sea_mask.reshape(sea_tiles, LANES)

    offset = 6 * sea_tiles
    feed_rows = 2 * air_sources.shape[0] * sea_tiles
    smalls = [tile_rows(v) for v in (ocean_sources, ocean_weights, surface_forcing)]
    feeds = [tile_rows(v) for v in (air_sources, air_weights)]
    hbm = pltpu.HBM
    vmem = lambda v: pltpu.VMEM(v.shape, v.dtype)
    (top,) = call(first_top, [((2 * sea_tiles, LANES), f32)], sea, ice, space=hbm,
                  scratch=[pltpu.VMEM((SUBS * sea_tiles, LANES), f32), pltpu.SemaphoreType.DMA((2,))])
    near = sec_exchange(top)
    code, fixed, feed, wet = call(
        lambda *r: first_rest(cols, secs, cells, here, *r),
        [((ko, tiles, LANES), i32), ((ko + 8, tiles, LANES), f32), ((feed_rows, LANES), f32), (wet.shape, i32)],
        air, *smalls, air_mask.reshape(tiles, LANES), *feeds, wet, space=hbm,
        scratch=[pltpu.VMEM((fields, SUBS * tiles, LANES), f32), *map(vmem, smalls), pltpu.VMEM((tiles, LANES), i32),
                 vmem(feeds[0]), pltpu.SemaphoreType.DMA((8,))],
    )
    ice = top[sea_tiles:]
    (bundle,) = call(first_bundle, [((offset + feed_rows, LANES), f32)], top, *near, feed)
    y2, hg, tops, sea, sea_k = call(
        air_prepare,
        [(air.shape, f32), ((2,) + mixing.shape, f32), ((fields + 1, tiles, LANES), f32), (sea.shape, f32), (sea_k.shape, f32)],
        air, mixing, sea, sea_k, space=hbm,
        scratch=[vmem(air), vmem(mixing), pltpu.VMEM((3, levels, tiles, LANES), f32),
                 pltpu.VMEM((fields + 1, levels, tiles, LANES), f32), pltpu.VMEM((fields + 1, levels, tiles, LANES), f32),
                 pltpu.SemaphoreType.DMA((fields + 3,))],
    )
    bundles = col_exchange([bundle] * cols)
    adds, tables = [], bundles
    for step in range(STEPS):
        extra = (tops, adds[0]) if step else ()
        flux, add = call(
            lambda *r: flux_kernel(bool(step), cols, sea_tiles, *r),
            [((FLUXES * tiles, LANES), f32), ((fields, tiles, LANES), f32)],
            *tables, code, fixed, *extra,
        )
        adds.append(add)
        near = sec_exchange(flux)
        share = ((FLUXES * sea_tiles, LANES), f32)
        sums = lambda slots, peers, *args: call(
            lambda *r: partial_kernel(offset, slots, len(peers), *r), [share] * len(peers), *args)
        parts = sums((0,), bundles[1:], flux, *bundles[1:])
        parts = sums((1,), bundles[1:], near[0], *bundles[1:], *parts)
        parts = sums((2,), bundles[1:], near[1], *bundles[1:], *parts)
        moved = col_exchange([flux, *parts])
        moved[:1] = sums((0, 1, 2), bundles[:1], flux, *near, bundles[0])
        last = step == STEPS - 1
        if last:
            (air_out,) = call(air_finish, [(air.shape, f32)], y2, hg, *adds, out_space=None)
        solve_scratch = [pltpu.VMEM((3, depth, sea_tiles, LANES), f32), pltpu.VMEM((2, depth, sea_tiles, LANES), f32)]
        sea, top = call(
            lambda *r: sea_kernel(cols, depth, last, *r),
            [(sea.shape, f32), ((sea_tiles if last else 2 * sea_tiles, LANES), f32)],
            *moved, sea, sea_k, ice, wet, out_space=hbm if last else pltpu.VMEM,
            scratch=solve_scratch + ([vmem(sea), vmem(ice), pltpu.SemaphoreType.DMA((3,))] if last else []),
        )
        if not last:
            ice = top[sea_tiles:]
            (bundle,) = call(later_bundle, [((offset, LANES), f32)], top, *sec_exchange(top))
            tables = col_exchange([bundle] * cols)
    return (untile_rows(air_out, levels, here), untile_rows(sea, depth, cells), top.reshape(cells))


def solution(mesh):
    both = ("sec", "col")
    placed = (
        P(None, None, both), P(None, both), P(None, both), P(both), P(None, both), P(None, both),
        P(None, None, both), P(None, both), P(both), P(both), P(None, both), P(None, both),
    )
    return jax.shard_map(
        per_device,
        mesh=mesh,
        in_specs=placed,
        out_specs=(P(None, None, both), P(None, None, both), P(both)),
        check_vma=False,
    )
```

```python
import math

import jax
import jax.numpy as jnp
from jax import lax
from jax.experimental import pallas as pl
from jax.experimental.pallas import tpu as pltpu
from jax.sharding import PartitionSpec as P


STEPS = 2
LANES = 128
SUBS = 8
FLUXES = 5


def tile_rows(x):
    *lead, r, n = x.shape
    t = min(r, SUBS)
    y = x.reshape(*lead, r // t, t, n // LANES, LANES)
    return jnp.swapaxes(y, -3, -2).reshape(*lead, r * n // LANES, LANES)


def untile_rows(x, r, n):
    lead = x.shape[:-2]
    t = min(r, SUBS)
    y = x.reshape(*lead, r // t, n // LANES, t, LANES)
    return jnp.swapaxes(y, -3, -2).reshape(*lead, r, n)


def level_rows(level, tiles, height=SUBS):
    return pl.ds((level // height) * height * tiles + level % height, tiles, stride=height)


def split(x, size):
    if size & (size - 1) == 0:
        return x >> (size.bit_length() - 1), x & (size - 1)
    return x // size, x % size


def sec_partners():
    n = lax.axis_size("sec")
    if n % 2 == 0:
        return (
            [(i, i ^ 1) for i in range(n)],
            [(i, (i + 1) % n if i % 2 else (i - 1) % n) for i in range(n)],
        )
    return ([(i, (i + 1) % n) for i in range(n)], [(i, (i - 1) % n) for i in range(n)])


def section_slot(band, sec, n):
    odd = sec & 1 if n % 2 == 0 else 1
    return jnp.where(band == 1, 0, jnp.where((band == 0) == (odd == 1), 1, 2))


def col_pairs(j):
    n = lax.axis_size("col")
    if n & (n - 1) == 0:
        return [(i, i ^ j) for i in range(n)]
    return [(i, (i + j) % n) for i in range(n)]


def row_slot(owner, col, n):
    if n & (n - 1) == 0:
        return owner ^ col
    rest = col - owner
    return jnp.where(rest < 0, rest + n, rest)


def slot_section(slot, sec, n):
    if slot == 0:
        return sec
    if n % 2 == 0:
        step = jnp.where((sec & 1) == (slot & 1), -1, 1)
    else:
        step = -1 if slot == 1 else 1
    at = sec + step
    return jnp.where(at < 0, at + n, jnp.where(at >= n, at - n, at))


def slot_row(j, col, n):
    if n & (n - 1) == 0:
        return col ^ j
    at = col - j
    return jnp.where(at < 0, at + n, at)


def sec_exchange(x):
    got = []
    for pairs in sec_partners():
        got.append(lax.ppermute(x, "sec", pairs))
    return got


def col_exchange(pieces):
    got = [pieces[0]]
    for j in range(1, len(pieces)):
        got.append(lax.ppermute(pieces[j], "col", col_pairs(j)))
    return got


def factor(mix, depth, put):
    half = depth // 2
    one = jnp.ones_like(mix(0))
    sides = []
    for side in (0, 1):
        if side == 0:
            sides.append([one, one, None])
        else:
            sides.append([one + mix(depth - 1), one, None])
    scale = [None, None]
    last = [None, None]
    for step in range(half):
        for side in (0, 1):
            n, d, _ = sides[side]
            i = step if side == 0 else depth - 1 - step
            ahead = mix(i) if side == 0 else mix(i - 1)
            behind = None
            if step:
                behind = mix(i - 1) if side == 0 else mix(i)
            d1 = n + ahead * d
            r1 = 1.0 / d1
            inv = d * r1
            n1 = d1 + ahead * n
            if step % 4 == 3:
                d1, n1 = d1 * scale[side], n1 * scale[side]
            if step % 4 == 0:
                scale[side] = r1
            out = ahead * inv
            put(i, inv, out, None if behind is None else behind * inv)
            sides[side] = [n1, d1, None]
            last[side] = out
    return 1.0 / (1.0 - last[0] * last[1])


def apply_factor(rhs, depth, get, middle, keep, kept, store):
    half = depth // 2
    carry = [None, None]
    for step in range(half):
        for side in (0, 1):
            i = step if side == 0 else depth - 1 - step
            inv, _, back = get(i)
            r = rhs(i)
            value = None if r is None else r * inv
            if step and carry[side] is not None:
                moved = back * carry[side]
                value = moved if value is None else value + moved
            carry[side] = value
            if value is not None:
                keep(i, value)
    top, bottom = carry
    up, down = get(half - 1)[1], get(half)[1]
    x_top = (top if bottom is None else top + up * bottom) * middle
    x_bottom = down * x_top if bottom is None else bottom + down * x_top
    store(half - 1, x_top)
    store(half, x_bottom)
    xs = [x_top, x_bottom]
    for step in range(half - 2, -1, -1):
        for side in (0, 1):
            i = step if side == 0 else depth - 1 - step
            x = get(i)[1] * xs[side]
            if side == 0 or bottom is not None:
                x = x + kept(i)
            xs[side] = x
            store(i, x)


def fetch(pairs, sems):
    copies = [pltpu.make_async_copy(src, dst, sems.at[i]) for i, (src, dst) in enumerate(pairs)]
    for c in copies:
        c.start()
    return copies


def first_top(sea_hbm, ice_hbm, top_ref, sea0, sems):
    n = ice_hbm.shape[0]
    copies = fetch([(sea_hbm.at[0, pl.ds(0, SUBS * n)], sea0), (ice_hbm, top_ref.at[pl.ds(n, n)])], sems)
    for c in copies:
        c.wait()
    top_ref[0:n] = sea0[level_rows(0, n), :]


def first_rest(cols, secs, cells_here, cols_here,
               air_hbm, src_hbm, w_hbm, forcing_hbm, mask_hbm, feed_hbm, feed_w_hbm, wet_hbm,
               code_ref, fixed_ref, feed_ref, wet_ref,
               air0, src_ref, w_ref, forcing_ref, mask_ref, feed_in, sems):
    tiles = mask_ref.shape[0]
    m = feed_in.shape[0]
    sec, col = lax.axis_index("sec"), lax.axis_index("col")
    copies = fetch(
        [(feed_hbm, feed_in), (feed_w_hbm, feed_ref.at[pl.ds(m, m)]),
         (src_hbm, src_ref), (w_hbm, w_ref), (forcing_hbm, forcing_ref), (mask_hbm, mask_ref), (wet_hbm, wet_ref),
         (air_hbm.at[:, pl.ds(0, SUBS * tiles)], air0)], sems)
    for c in copies:
        c.wait()
    band, within = split(feed_in[...], cols_here * cols)
    owner, place = split(within, cols_here)
    code = (owner * 3 + section_slot(band, sec, secs)) * cols_here + place
    feed_ref[0:m] = code.astype(jnp.float32)

    mask = mask_ref[...] == 1
    ks = src_ref.shape[0] // tiles
    for k in range(ks):
        s = src_ref[pl.ds(k, tiles, stride=ks), :]
        band, within = split(s, cells_here * cols)
        owner, place = split(within, cells_here)
        slot = section_slot(band, sec, secs) * cols + row_slot(owner, col, cols)
        code_ref[k] = slot * cells_here + place
        fixed_ref[k] = jnp.where(mask, w_ref[pl.ds(k, tiles, stride=ks), :], 0.0)
    nf = forcing_ref.shape[0] // tiles
    for k in range(nf):
        f = forcing_ref[pl.ds(k, tiles, stride=nf), :]
        fixed_ref[ks + k] = f if k < nf - 1 else jnp.where(mask, 0.0, f)
    for f in range(air0.shape[0]):
        fixed_ref[ks + nf + f] = air0[f, level_rows(0, tiles), :]


def air_prepare(air_hbm, mix_hbm, sea_hbm, sea_mix_hbm, y2_ref, hg_ref, top_ref, sea_ref, sea_mix_ref,
                air_ref, mix_ref, fac, work, x1, sems):
    depth = fac.shape[1]
    tiles = mix_ref.shape[0] // depth
    fields = air_ref.shape[0]
    copies = fetch(
        [(mix_hbm, mix_ref)] + [(air_hbm.at[f], air_ref.at[f]) for f in range(fields)]
        + [(sea_hbm, sea_ref), (sea_mix_hbm, sea_mix_ref)], sems)
    copies[0].wait()

    def put(i, inv, out, back):
        fac[0, i] = inv
        fac[1, i] = out
        if back is not None:
            fac[2, i] = back

    middle = factor(lambda i: mix_ref[level_rows(i, tiles), :], depth, put)

    class Get:
        def __call__(self, i):
            return (fac[0, i], fac[1, i], fac[2, i])

    get = Get()
    for f in [fields] + list(range(fields)):
        if f < fields:
            copies[1 + f].wait()

        def rhs(i, f=f):
            if f < fields:
                return air_ref[f, level_rows(i, tiles), :]
            return jnp.ones_like(middle) if i == 0 else None

        def keep(i, v, f=f):
            work[f, i] = v

        def kept(i, f=f):
            return work[f, i]

        def store(i, v, f=f):
            x1[f, i] = v
            if f == fields:
                hg_ref[1, level_rows(i, tiles), :] = v

        apply_factor(rhs, depth, get, middle, keep, kept, store)
        top_ref[f] = x1[f, 0]
    for f in range(fields + 1):
        def rhs(i, f=f):
            return x1[f, i]

        def keep(i, v, f=f):
            work[f, i] = v

        def kept(i, f=f):
            return work[f, i]

        def store(i, v, f=f):
            if f < fields:
                y2_ref[f, level_rows(i, tiles), :] = v
            else:
                hg_ref[0, level_rows(i, tiles), :] = v

        apply_factor(rhs, depth, get, middle, keep, kept, store)
    for c in copies[1 + fields :]:
        c.wait()


def first_bundle(own_ref, m1_ref, m2_ref, feed_ref, out_ref):
    n = own_ref.shape[0]
    later_bundle(own_ref, m1_ref, m2_ref, out_ref.at[0 : 3 * n])
    out_ref[3 * n :] = feed_ref[...]


def later_bundle(own_ref, m1_ref, m2_ref, out_ref):
    n = own_ref.shape[0]
    out_ref[0:n] = own_ref[...]
    out_ref[n : 2 * n] = m1_ref[...]
    out_ref[2 * n : 3 * n] = m2_ref[...]


def lane_gather(row, lane):
    return jnp.take_along_axis(jnp.broadcast_to(row, lane.shape), lane, axis=1)


def look_up(codes, cell_rows, pieces, row):
    found = []
    for code in codes:
        hi, lane = split(code, LANES)
        vals = [jnp.zeros(lane.shape, jnp.float32) for _ in range(2)]
        for slot in range(3):
            for j in range(pieces):
                for r in range(cell_rows):
                    hit = hi == (slot * pieces + j) * cell_rows + r
                    for v in range(2):
                        vals[v] = jnp.where(hit, lane_gather(row(slot, j, v * cell_rows + r), lane), vals[v])
        found.append(vals)
    return found


def surface_fluxes(found, weights, forcing, bottom):
    short, long_, rain, skin = forcing
    frozen = jnp.zeros_like(skin)
    for w, vals in zip(weights, found):
        skin = skin + w * vals[0]
        frozen = frozen + w * vals[1]
    cover = 1.0 / (1.0 + frozen)
    speed = jnp.sqrt(bottom[2] * bottom[2] + bottom[3] * bottom[3] + 1.0)
    coefficient = 0.3 * speed * cover
    snow = 1.0 / (1.0 + jnp.exp(2.0 * skin))
    f0 = coefficient * (skin - bottom[0])
    f1 = coefficient * (0.5 * jnp.exp(0.3 * skin) - bottom[1])
    f2 = coefficient * bottom[2]
    f3 = coefficient * bottom[3]
    f4 = short * cover
    f5 = long_ - 0.2 * skin
    f6 = rain * (1.0 - snow)
    f7 = rain * snow
    return (f2, f3, f4 + f5 - f0 - f1, 0.4 * f1 - f6, f7), (f0, f1, -f2, -f3)


def put_rows(ref, values):
    n = values[0].shape[0]
    for v, value in enumerate(values):
        ref[v * n : (v + 1) * n] = value


def first_fluxes(pieces, cell_rows, *refs):
    tables, (code_ref, fixed_ref, top_ref, flux_ref, add_ref, pack_ref) = refs[:pieces], refs[pieces:]
    ks = code_ref.shape[0]
    found = look_up([code_ref[k] for k in range(ks)], cell_rows, pieces,
                    lambda slot, j, at: tables[j][slot * 2 * cell_rows + at : slot * 2 * cell_rows + at + 1, :])
    rows = [fixed_ref[i] for i in range(ks + 8)]
    flux, adds = surface_fluxes(found, rows[:ks], rows[ks : ks + 4], rows[ks + 4 :])
    put_rows(flux_ref, flux)
    for f, add in enumerate(adds):
        add_ref[f] = add
        pack_ref[f] = top_ref[f] + top_ref[4] * add
    for k in range(ks):
        pack_ref[4 + k] = code_ref[k].astype(jnp.float32)
    for i in range(ks + 4):
        pack_ref[4 + ks + i] = rows[i]


def packed_fluxes(pack_ref, cell_rows, pieces, row, flux_ref, add_ref):
    ks = (pack_ref.shape[0] - 8) // 2
    found = look_up([pack_ref[4 + k].astype(jnp.int32) for k in range(ks)], cell_rows, pieces, row)
    rows = [pack_ref[4 + ks + i] for i in range(ks + 4)]
    flux, adds = surface_fluxes(found, rows[:ks], rows[ks:], [pack_ref[f] for f in range(4)])
    put_rows(flux_ref, flux)
    if add_ref is not None:
        for f, add in enumerate(adds):
            add_ref[f] = add


def later_fluxes(pieces, cell_rows, *refs):
    tables, (pack_ref, flux_ref, add_ref) = refs[:pieces], refs[pieces:]
    packed_fluxes(pack_ref, cell_rows, pieces,
                  lambda slot, j, at: tables[j][slot * 2 * cell_rows + at : slot * 2 * cell_rows + at + 1, :],
                  flux_ref, add_ref)


def wide_fluxes(secs, cols, cell_rows, all_ref, *refs):
    packs, fluxes, add_ref = refs[:3], refs[3:6], refs[6]
    sec, col = lax.axis_index("sec"), lax.axis_index("col")
    for n in range(3):
        home = slot_section(n, sec, secs)
        owners = [slot_section(slot, home, secs) * cols for slot in range(3)]
        places = [slot_row(j, col, cols) for j in range(cols)]
        packed_fluxes(packs[n], cell_rows, cols,
                      lambda slot, j, at: all_ref[owners[slot] + places[j], at : at + 1, :],
                      fluxes[n], None if n else add_ref)


def partial_kernel(offset, slots, pieces, *refs):
    flux, refs = refs[: len(slots)], refs[len(slots) :]
    bundles, refs = refs[:pieces], refs[pieces:]
    before, outs = refs[:-pieces], refs[-pieces:]
    col_rows = flux[0].shape[0] // FLUXES
    base = lax.axis_index("col") * (3 * col_rows)
    m = outs[0].shape[0] // FLUXES
    ks = (bundles[0].shape[0] - offset) // 2 // m
    per = SUBS // m
    for j in range(pieces):
        total = [None] * FLUXES
        for q in range(ks // per):
            code, w = [], []
            for k in range(q * per, (q + 1) * per):
                code.append(bundles[j][pl.ds(offset + k, m, stride=ks), :])
                w.append(bundles[j][pl.ds(offset + ks * m + k, m, stride=ks), :])
            code = jnp.concatenate(code, axis=0).astype(jnp.int32)
            w = jnp.concatenate(w, axis=0)
            hi, lane = split(code, LANES)
            hi = hi - base
            vals = [jnp.zeros(lane.shape, jnp.float32) for _ in range(FLUXES)]
            for table, slot in zip(flux, slots):
                for r in range(col_rows):
                    hit = hi == slot * col_rows + r
                    for v in range(FLUXES):
                        row = table[v * col_rows + r : v * col_rows + r + 1, :]
                        vals[v] = jnp.where(hit, lane_gather(row, lane), vals[v])
            for v in range(FLUXES):
                part = w * vals[v]
                total[v] = part if total[v] is None else total[v] + part
        for v in range(FLUXES):
            at = slice(v * m, (v + 1) * m)
            whole = total[v][0:m]
            for p in range(1, per):
                whole = whole + total[v][p * m : (p + 1) * m]
            outs[j][at] = whole + before[j][at] if before else whole


def sea_kernel(pieces, depth, last, spread, *refs):
    parts, refs = refs[:pieces], refs[pieces:]
    state_ref, mix_ref, ice_ref, mask_ref, refs = refs[0], refs[1], refs[2], refs[3], refs[4:]
    if last:
        out_hbm, top_hbm, fac, work, out_ref, top_ref, sems = refs
    elif spread:
        out_ref, top_ref, all_ref, fac, work = refs
    else:
        out_ref, top_ref, fac, work = refs
    tiles = mix_ref.shape[0] // depth
    flux = []
    for v in range(FLUXES):
        total = parts[0][v * tiles : (v + 1) * tiles]
        for p in parts[1:]:
            total = total + p[v * tiles : (v + 1) * tiles]
        flux.append(total)
    ice = ice_ref[...]
    wet = mask_ref[...] == 1
    stress2 = 2.0 * jnp.sqrt(flux[0] * flux[0] + flux[1] * flux[1] + 0.01)
    heat, salt, snow = flux[2], flux[3], flux[4]
    open_water = 1.0 - ice
    adds = (0.5 * open_water * heat, 0.3 * open_water * salt)
    grown = ice / (ice + open_water * jnp.exp(0.5 * heat - 0.8 * snow))
    new_ice = jnp.where(wet, grown, ice)

    known = {}

    def mix(i):
        if i not in known:
            k = mix_ref[level_rows(i, tiles), :]
            known[i] = k * (1.0 + stress2 * math.exp(-i / 8.0))
        return known[i]

    def put(i, inv, out, back):
        fac[0, i] = inv
        fac[1, i] = out
        if back is not None:
            fac[2, i] = back

    copies = []
    if last:
        top_ref[...] = new_ice
        copies.append(pltpu.make_async_copy(top_ref, top_hbm, sems.at[2]))
        copies[-1].start()
    else:
        top_ref[tiles : 2 * tiles] = new_ice
    middle = factor(mix, depth, put)
    for f in range(2):
        def rhs(i, f=f):
            r = state_ref[f, level_rows(i, tiles), :]
            return r + adds[f] if i == 0 else r

        def keep(i, v, f=f):
            work[f, i] = v

        def kept(i, f=f):
            return work[f, i]

        def store(i, v, f=f):
            new = jnp.where(wet, v, state_ref[f, level_rows(i, tiles), :])
            out_ref[f, level_rows(i, tiles), :] = new
            if f == 0 and i == 0 and not last:
                top_ref[0:tiles] = new

        apply_factor(rhs, depth, lambda i: (fac[0, i], fac[1, i], fac[2, i]), middle, keep, kept, store)
        if last:
            copies.append(pltpu.make_async_copy(out_ref.at[f], out_hbm.at[f], sems.at[f]))
            copies[-1].start()
    for c in copies:
        c.wait()
    if spread:
        for i in range(all_ref.shape[0]):
            all_ref[i] = top_ref[...]


def air_finish(y2_ref, hg_ref, first_ref, second_ref, out_ref):
    fields, tiles = first_ref.shape[0], first_ref.shape[1]
    rows = y2_ref.shape[1]
    for f in range(fields):
        for j in range(tiles):
            b1 = jnp.broadcast_to(first_ref[f, j : j + 1, :], (SUBS, LANES))
            b2 = jnp.broadcast_to(second_ref[f, j : j + 1, :], (SUBS, LANES))
            for t in range(rows // (SUBS * tiles)):
                at = slice((t * tiles + j) * SUBS, (t * tiles + j + 1) * SUBS)
                out_ref[f, at] = y2_ref[f, at] + hg_ref[0, at] * b1 + hg_ref[1, at] * b2


def call(kernel, out, *args, scratch=(), out_space=pltpu.VMEM, space=pltpu.VMEM):
    spaces = out_space if isinstance(out_space, list) else [out_space] * len(out)
    return pl.pallas_call(
        kernel,
        out_shape=[pltpu.VMEM(*o) if sp is pltpu.VMEM else jax.ShapeDtypeStruct(*o) for o, sp in zip(out, spaces)],
        in_specs=[pl.BlockSpec(memory_space=space)] * len(args),
        out_specs=[pl.BlockSpec(memory_space=sp or pltpu.VMEM) for sp in spaces],
        scratch_shapes=list(scratch),
        compiler_params=pltpu.CompilerParams(vmem_limit_bytes=8 << 20),
    )(*[pltpu.with_memory_space_constraint(a, space) for a in args])


def per_device(air_state, air_mix, surface_forcing, air_mask, ocean_sources, ocean_weights,
               sea_state, sea_mix, ice_cover, sea_mask, air_sources, air_weights):
    cols, secs = lax.axis_size("col"), lax.axis_size("sec")
    fields, levels, here = air_state.shape
    depth, cells = sea_mix.shape
    tiles, sea_tiles = here // LANES, cells // LANES
    f32, i32 = jnp.float32, jnp.int32
    ko = ocean_sources.shape[0]

    air = tile_rows(air_state)
    mixing = tile_rows(air_mix)
    sea = tile_rows(sea_state)
    sea_k = tile_rows(sea_mix)
    ice = ice_cover.reshape(sea_tiles, LANES)
    wet = sea_mask.reshape(sea_tiles, LANES)

    offset = 6 * sea_tiles
    feed_rows = 2 * air_sources.shape[0] * sea_tiles
    smalls = [tile_rows(v) for v in (ocean_sources, ocean_weights, surface_forcing)]
    feeds = [tile_rows(v) for v in (air_sources, air_weights)]
    hbm = pltpu.HBM
    vmem = lambda v: pltpu.VMEM(v.shape, v.dtype)
    (top,) = call(first_top, [((2 * sea_tiles, LANES), f32)], sea, ice, space=hbm,
                  scratch=[pltpu.VMEM((SUBS * sea_tiles, LANES), f32), pltpu.SemaphoreType.DMA((2,))])
    near = sec_exchange(top)
    code, fixed, feed, wet = call(
        lambda *r: first_rest(cols, secs, cells, here, *r),
        [((ko, tiles, LANES), i32), ((ko + 8, tiles, LANES), f32), ((feed_rows, LANES), f32), (wet.shape, i32)],
        air, *smalls, air_mask.reshape(tiles, LANES), *feeds, wet, space=hbm,
        scratch=[pltpu.VMEM((fields, SUBS * tiles, LANES), f32), *map(vmem, smalls), pltpu.VMEM((tiles, LANES), i32),
                 vmem(feeds[0]), pltpu.SemaphoreType.DMA((8,))],
    )
    ice = top[sea_tiles:]
    (bundle,) = call(first_bundle, [((offset + feed_rows, LANES), f32)], top, *near, feed)
    y2, hg, tops, sea, sea_k = call(
        air_prepare,
        [(air.shape, f32), ((2,) + mixing.shape, f32), ((fields + 1, tiles, LANES), f32), (sea.shape, f32), (sea_k.shape, f32)],
        air, mixing, sea, sea_k, space=hbm,
        scratch=[vmem(air), vmem(mixing), pltpu.VMEM((3, levels, tiles, LANES), f32),
                 pltpu.VMEM((fields + 1, levels, tiles, LANES), f32), pltpu.VMEM((fields + 1, levels, tiles, LANES), f32),
                 pltpu.SemaphoreType.DMA((fields + 3,))],
    )
    bundles = col_exchange([bundle] * cols)
    wide = cols * secs <= 64
    adds, tables = [], bundles
    flux_out = ((FLUXES * tiles, LANES), f32)
    add_out = ((fields, tiles, LANES), f32)
    share = ((FLUXES * sea_tiles, LANES), f32)

    def sums(slots, peers, *args):
        return call(lambda *r: partial_kernel(offset, slots, len(peers), *r), [share] * len(peers), *args)

    for step in range(STEPS):
        last = step == STEPS - 1
        peers = bundles[1:]
        if step and wide:
            flux, *near, add = call(
                lambda *r: wide_fluxes(secs, cols, sea_tiles, *r), [flux_out] * 3 + [add_out], everywhere, pack, *halo
            )
            parts = sums((0, 1, 2), peers, flux, *near, *peers)
        else:
            if step:
                flux, add = call(lambda *r: later_fluxes(cols, sea_tiles, *r), [flux_out, add_out], *tables, pack)
            else:
                flux, add, pack = call(
                    lambda *r: first_fluxes(cols, sea_tiles, *r),
                    [flux_out, add_out, ((2 * ko + 8, tiles, LANES), f32)], *tables, code, fixed, tops,
                )
            near = sec_exchange(flux)
            parts = sums((0,), peers, flux, *peers)
            parts = sums((1,), peers, near[0], *peers, *parts)
            parts = sums((2,), peers, near[1], *peers, *parts)
        adds.append(add)
        moved = col_exchange([flux, *parts])
        moved[:1] = sums((0, 1, 2), bundles[:1], flux, *near, bundles[0])
        if last:
            (air_out,) = call(air_finish, [(air.shape, f32)], y2, hg, *adds, out_space=None)
        elif wide:
            halo = sec_exchange(pack)
        spread = wide and not last
        sea, top, *rest = call(
            lambda *r: sea_kernel(cols, depth, last, spread, *r),
            [(sea.shape, f32), ((sea_tiles if last else 2 * sea_tiles, LANES), f32)]
            + [((secs * cols, 2 * sea_tiles, LANES), f32)] * spread,
            *moved, sea, sea_k, ice, wet, out_space=hbm if last else pltpu.VMEM,
            scratch=[pltpu.VMEM((3, depth, sea_tiles, LANES), f32), pltpu.VMEM((2, depth, sea_tiles, LANES), f32)]
            + ([vmem(sea), vmem(ice), pltpu.SemaphoreType.DMA((3,))] if last else []),
        )
        if not last:
            ice = top[sea_tiles:]
            if wide:
                ready, *halo = lax.optimization_barrier((rest[0], *halo))
                everywhere = lax.all_to_all(ready, ("sec", "col"), 0, 0)
            else:
                (bundle,) = call(later_bundle, [((offset, LANES), f32)], top, *sec_exchange(top))
                tables = col_exchange([bundle] * cols)
    return (untile_rows(air_out, levels, here), untile_rows(sea, depth, cells), top.reshape(cells))


def solution(mesh):
    both = ("sec", "col")
    placed = (
        P(None, None, both), P(None, both), P(None, both), P(both), P(None, both), P(None, both),
        P(None, None, both), P(None, both), P(both), P(both), P(None, both), P(None, both),
    )
    return jax.shard_map(
        per_device,
        mesh=mesh,
        in_specs=placed,
        out_specs=(P(None, None, both), P(None, None, both), P(both)),
        check_vma=False,
    )
```
